32 devices in a mesh: sec: 8 (over z, core), bond: 4 (over y, x).
Axes of the slice: x: 2, y: 2, z: 4, core: 2. Of those that a mesh axis runs over, the one named last changes fastest.
Arguments:
- left_env: bfloat16 [8, 512, 8, 512], P('sec', 'bond'), may hold values from -6 to 6
- site: bfloat16 [8, 512, 4, 512], P('sec', 'bond'), may hold values from -0.125 to 0.125
- psi: bfloat16 [8, 512, 4, 4, 512], P('sec', 'bond'), may hold values from -0.25 to 0.25
- right_env: bfloat16 [8, 8, 512, 512], P('sec'), may hold values from -0.09375 to 0.09375
- mpo: bfloat16 [8, 8, 4, 4], replicated, may hold values from -1 to 1
Outputs:
- new_left: bfloat16 [8, 512, 8, 512], P('sec', 'bond')
- product: bfloat16 [8, 512, 4, 4, 512], P('sec', 'bond')
The draws below stay inside these ranges and needn't reach their ends.
All inputs are finite; a program needn't handle non-finite values.
Results may differ from the reference program's by a relative error of at most 0.0095.
Values may be sent and summed in bfloat16 or wider, within the bound.
A program may use at most 128 MiB of HBM per device.

```python
import jax
import jax.numpy as jnp
from jax import lax

CHI = 512
MPO_W = 8
PHYS = 4
SECTIONS = 8


def level_of(stream_key, extent, cuts, low, high):
    factor_of = 1.0
    for dim, parts in cuts:
        heights = jax.random.uniform(jax.random.fold_in(jax.random.fold_in(stream_key, 6), dim), (parts,), jnp.float32, low / len(cuts), high / len(cuts))
        factor_of = factor_of * jnp.repeat(jnp.exp(heights), extent[dim] // parts).reshape((-1,) + (1,) * (len(extent) - 1 - dim))
    return factor_of


def gaussian(key, shape, spread, reach, pieces=(), held_as=jnp.bfloat16):
    drawn = jax.random.normal(key, shape, jnp.float32) * spread
    if len(pieces) > 0:
        drawn = level_of(key, shape, pieces, -0.22, 0.18) * drawn
    return jnp.clip(drawn, min=-reach, max=reach).astype(held_as)


def setup_inputs(seed: int = 0) -> dict:
    arg_keys = jax.random.split(jax.random.key(seed), 6)
    return {
        "left_env": gaussian(arg_keys[0], (SECTIONS, CHI, MPO_W, CHI), 1.0, 6.0, ((0, 8), (1, 4))),
        "site": gaussian(arg_keys[1], (SECTIONS, CHI, PHYS, CHI), (CHI * PHYS) ** -0.5, 0.125, ((0, 8), (1, 4))),
        "psi": gaussian(arg_keys[2], (SECTIONS, CHI, PHYS, PHYS, CHI), CHI ** -0.5, 0.25, ((0, 8), (1, 4))),
        "right_env": gaussian(arg_keys[3], (SECTIONS, MPO_W, CHI, CHI), (MPO_W * CHI) ** -0.5, 0.09375, ((0, 8),)),
        "mpo": gaussian(arg_keys[4], (MPO_W, MPO_W, PHYS, PHYS), (MPO_W * PHYS) ** -0.5, 1.0),
    }


def reference(left_env, site, psi, right_env, mpo):
    mpo_wide = mpo.astype(jnp.float32)

    def update(pair):
        left, tensor = pair
        first = jnp.dot(left.reshape(CHI * MPO_W, CHI), tensor.reshape(CHI, PHYS * CHI), preferred_element_type=jnp.float32)
        first = first.astype(jnp.bfloat16).reshape(CHI, MPO_W, PHYS, CHI)
        second = jnp.einsum("pmsb,mnsu->punb", first.astype(jnp.float32), mpo_wide).astype(jnp.bfloat16)
        fresh = jnp.dot(tensor.reshape(CHI * PHYS, CHI).T, second.reshape(CHI * PHYS, MPO_W * CHI), preferred_element_type=jnp.float32)
        return fresh.astype(jnp.bfloat16).reshape(CHI, MPO_W, CHI)

    new_left = lax.map(update, (left_env, site))
    two_site = jnp.einsum("mnsu,nkvw->msvuwk", mpo_wide, mpo_wide).astype(jnp.bfloat16).reshape(MPO_W * PHYS * PHYS, PHYS * PHYS * MPO_W)

    def apply(triple):
        left, pair, right = triple
        mixed = jnp.dot(left.reshape(CHI * MPO_W, CHI), pair.reshape(CHI, PHYS * PHYS * CHI), preferred_element_type=jnp.float32)
        mixed = mixed.astype(jnp.bfloat16).reshape(CHI, MPO_W * PHYS * PHYS, CHI)
        projected = jnp.einsum("pqc,qr->prc", mixed.astype(jnp.float32), two_site.astype(jnp.float32)).astype(jnp.bfloat16)
        result = jnp.dot(projected.reshape(CHI * PHYS * PHYS, MPO_W * CHI), right.reshape(MPO_W * CHI, CHI), preferred_element_type=jnp.float32)
        return result.astype(jnp.bfloat16).reshape(CHI, PHYS, PHYS, CHI)

    product = lax.map(apply, (jnp.roll(new_left, 1, axis=0), jnp.roll(psi, 1, axis=0), right_env))
    return new_left, product
```

```python
import functools

import jax
import jax.numpy as jnp
from jax import lax
from jax.experimental import pallas as pl
from jax.experimental.pallas import tpu as pltpu
from jax.sharding import PartitionSpec as P

MESH = pl.DeviceIdType.MESH
BF16 = jnp.bfloat16
F32 = jnp.float32


def mm(a, b):
    return jnp.dot(a, b, preferred_element_type=F32)


def kernel(
    dims,
    left_h, site_h, psi_h, right_h, mpo_h,
    new_left, product,
    left, site_raw, psi_raw, mpo, right,
    site_own, psi_own, site, site_tr, mix, pair,
    second, part, rs1, send2, rs2, nl_own, nl_out, nl_in, psi, mixed, proj, prod, acc,
    local_sem, send_sem, recv_sem,
):
    rows, width, phys, chi, group, cuts, batch = dims
    pq = phys * phys
    n_sec = lax.axis_size("sec")
    sec = lax.axis_index("sec")
    me = lax.axis_index("bond")
    x, y = lax.rem(me, 2), me // 2
    core, z = lax.rem(sec, 2), sec // 2
    mate_sec = 2 * z + 1 - core
    side_bond = 2 * y + 1 - x
    to_c = {"sec": mate_sec}
    to_y = {"bond": 2 * (1 - y) + x}
    to_x = {"bond": side_bond}
    to_xc = {"sec": mate_sec, "bond": side_bond}
    up = lax.rem(sec + 2, n_sec)
    to_up = {"sec": up}
    stays = x == core
    moves = x != core
    shifts = x == 1
    rests = x == 0

    mine = 2 * y + core
    mates = 2 * y + 1 - core
    across = 2 * (1 - y) + core
    corner = 2 * (1 - y) + 1 - core

    def block(owner):
        return pl.ds(pl.multiple_of(owner * rows, rows), rows)

    loads = {}
    for i, (name, src, dst) in enumerate((
        ("site", site_h, site_raw),
        ("psi", psi_h, psi_raw),
        ("mpo", mpo_h, mpo),
    )):
        loads[name] = pltpu.make_async_copy(src, dst, local_sem.at[i])
        loads[name].start()

    barrier = pltpu.get_barrier_semaphore()
    greeted = [to_c, to_y, to_x, to_xc]
    for dz in (2, n_sec - 2):
        greeted.append({"sec": lax.rem(sec + dz, n_sec)})
        greeted.append({"sec": lax.rem(mate_sec + dz, n_sec), "bond": side_bond})
    for target in greeted:
        pl.semaphore_signal(barrier, inc=1, device_id=target, device_id_type=MESH)
    pl.semaphore_wait(barrier, len(greeted))

    started = {}
    counter = {}

    def slot(key):
        return counter.setdefault(key, len(counter))

    def remote(i, j, src, dst, target):
        return pltpu.make_async_remote_copy(
            src_ref=src, dst_ref=dst, send_sem=send_sem.at[i], recv_sem=recv_sem.at[j],
            device_id=target, device_id_type=MESH,
        )

    def send(key, src, dst, target, when=None, land=None):
        i = slot(key)
        copy = remote(i, i if land is None else land, src, dst, target)
        if when is None:
            copy.start()
        else:
            pl.when(when)(copy.start)
        started.setdefault(key, []).append((copy, when))

    def keep(key, src, dst, when, land=None):
        copy = pltpu.make_async_copy(src, dst, recv_sem.at[slot(key) if land is None else land])
        pl.when(when)(copy.start)

    def arrive(key, dst, land=None):
        i = slot(key)
        remote(i, i if land is None else land, dst, dst, to_c).wait_recv()

    lanes = chi // cuts
    halves = (pl.ds(0, phys // 2), pl.ds(phys // 2, phys - phys // 2))
    n_left = 4
    tall_left = rows // n_left

    def left_part(i):
        return pl.ds(i * tall_left, tall_left)

    def send_left(i):
        send(("left", i), left_h.at[left_part(i)], left.at[left_part(i)], to_xc, when=moves)
        keep(("left", i), left_h.at[left_part(i)], left.at[left_part(i)], stays)

    loads["site"].wait()
    flat = site_raw[...].astype(F32).reshape(rows * phys, chi)
    for i in range(cuts):
        acc[i, :rows * phys, :] = flat[:, i * lanes:(i + 1) * lanes]
    for t in range(phys):
        for i in range(cuts):
            tile = acc[i, pl.ds(t, rows, stride=phys), :]
            site_own[t, :, i * lanes:(i + 1) * lanes] = tile.astype(BF16)

    def site_spread(p, from_own):
        src = site_own.at[halves[p]] if from_own else site.at[halves[p], block(mine), :]
        when = stays if from_own else None
        send(("site_y", p), src, site.at[halves[p], block(mine), :], to_y, when)
        send(("site_c", p), src, site.at[halves[p], block(mine), :], to_c, when)

    for p in range(2):
        send(("site", p), site_own.at[halves[p]], site.at[halves[p], block(me), :], to_xc, when=moves)
        keep(("site", p), site_own.at[halves[p]], site.at[halves[p], block(me), :], stays)
        site_spread(p, True)
    for i in range(n_left):
        send_left(i)

    loads["psi"].wait()
    tall = 8

    @pl.loop(0, rows // tall)
    def _(g):
        flat = psi_raw[pl.ds(pl.multiple_of(g * tall, tall), tall)].astype(F32)
        flat = flat.reshape(tall * pq, chi)
        where = pl.ds(pl.multiple_of(g * tall * pq, tall * pq), tall * pq)
        for i in range(cuts):
            acc[i, where, :] = flat[:, i * lanes:(i + 1) * lanes]

    def region(q, owner):
        return psi.at[q, :, block(owner), :]

    psi_self = jnp.logical_and(x == 0, core == 0)
    psi_goes = jnp.logical_not(psi_self)
    to_psi = {
        "sec": lax.rem(2 * z + x + 2 * core, n_sec),
        "bond": 2 * y + core,
    }

    def launch(q):
        send(("own", q), psi_own.at[q], region(q, me), to_psi, when=psi_goes)
        keep(("own", q), psi_own.at[q], region(q, me), psi_self)

    for q in range(cuts):
        for t in range(pq):
            at = (t % 2) * lanes
            tile = acc[q, pl.ds(t, rows, stride=pq), :]
            psi_own[q, t // 2, :, at:at + lanes] = tile.astype(BF16)
        if 0 < q < 3:
            launch(q - 1)

    send("right", right_h, right, to_c, when=moves)
    keep("right", right_h, right, moves)

    def spread(q):
        arrive(("own", q), region(q, mine))
        send(("psi_y", q), region(q, mine), region(q, mine), to_y)
        send(("psi_c", q), region(q, mine), region(q, mine), to_c)

    def relay(q):
        arrive(("psi_y", q), region(q, across))
        send(("psi_yc", q), region(q, across), region(q, across), to_c)

    def complete(q):
        arrive(("psi_c", q), region(q, mates))
        arrive(("psi_yc", q), region(q, corner))

    @pl.when(moves)
    def _():
        for p in range(2):
            arrive(("site", p), site.at[halves[p], block(mine), :])
            src = site.at[halves[p], block(mine), :]
            remote(slot(("site_y", p)), slot(("site_y", p)), src, src, to_y).start()
            remote(slot(("site_c", p)), slot(("site_c", p)), src, src, to_c).start()

    @pl.when(stays)
    def _():
        for p in range(2):
            arrive(("site", p), site.at[halves[p], block(mine), :])

    for p in range(2):
        for key, target in (("site_y", to_y), ("site_c", to_c)):
            src = site.at[halves[p], block(mine), :]
            i = slot((key, p))
            started[(key, p)] = [(remote(i, i, src, src, target), None)]

    loads["mpo"].wait()

    def iota(shape, axis):
        return lax.broadcasted_iota(jnp.int32, shape, axis)

    def one_hot(condition):
        return jnp.where(condition, 1.0, 0.0).astype(BF16)

    small = phys * width
    big = small * group
    tall_code = lax.div(iota((big, small), 0), group)
    spread_rows = one_hot(tall_code == iota((big, small), 1))
    col = iota((small, big), 1)
    col_code = lax.div(col, group * width) * width + lax.rem(col, width)
    spread_cols = one_hot(col_code == iota((small, big), 0))
    wide = mm(mm(spread_rows, mpo[...]).astype(BF16), spread_cols)
    same = lax.rem(iota((big, big), 0), group) == lax.rem(lax.div(iota((big, big), 1), width), group)
    mix[...] = jnp.where(same, wide, 0.0).astype(BF16)

    for t in range(phys):
        own = site[t, block(mine), :].astype(F32)
        for i in range(cuts):
            tile = own[:, i * lanes:(i + 1) * lanes]
            site_tr[i * lanes:(i + 1) * lanes, t * rows:(t + 1) * rows] = tile.T.astype(BF16)

    for p in range(2):
        arrive(("site_y", p), site.at[halves[p], block(across), :])
        send(("site_yc", p), site.at[halves[p], block(across), :], site.at[halves[p], block(across), :], to_c)

    def early(q):
        @pl.when(stays)
        def _():
            arrive(("own", q), region(q, mine))
            for key, target in (("psi_y", to_y), ("psi_c", to_c)):
                i = slot((key, q))
                remote(i, i, region(q, mine), region(q, mine), target).start()

    def late(q):
        @pl.when(moves)
        def _():
            arrive(("own", q), region(q, mine))
            for key, target in (("psi_y", to_y), ("psi_c", to_c)):
                i = slot((key, q))
                remote(i, i, region(q, mine), region(q, mine), target).start()
        for key, target in (("psi_y", to_y), ("psi_c", to_c)):
            i = slot((key, q))
            started[(key, q)] = [(remote(i, i, region(q, mine), region(q, mine), target), None)]

    early(0)
    for p in range(2):
        arrive(("site_c", p), site.at[halves[p], block(mates), :])
        arrive(("site_yc", p), site.at[halves[p], block(corner), :])

    strip = group * width
    per_left = tall_left // group

    for i in range(n_left):
        arrive(("left", i), left.at[left_part(i)])

        @pl.loop(i * per_left, (i + 1) * per_left)
        def _(g):
            ours = left[pl.ds(pl.multiple_of(g * group, group), group)].astype(F32)
            ours = ours.reshape(strip, chi).astype(BF16)
            first = jnp.concatenate([mm(ours, site[s]).astype(BF16) for s in range(phys)], axis=0)
            out = mm(mix[...], first).astype(BF16)
            for u in range(phys):
                for n in range(width):
                    at = (u * width + n) * group
                    where = pl.multiple_of(u * rows + g * group, group)
                    second[n, pl.ds(where, group), :] = out[at:at + group, :]

        if i == 1:
            early(1)

    launch(2)

    hrows = rows // 2

    def rows_of(stage, far, half):
        yy = 1 - y if far else y
        column = 1 - x if stage == 0 else x
        start = (2 * yy + column) * rows + half * hrows
        return pl.ds(pl.multiple_of(start, hrows), hrows)

    def block_of(stage, far):
        yy = 1 - y if far else y
        column = 1 - x if stage == 0 else x
        return block(2 * yy + column)

    def partial(stage):
        for far in (1, 0):
            where = block_of(stage, far)
            for n in range(width):
                part[n, where, :] = mm(site_tr[where, :], second[n]).astype(BF16)

    def swap_halves(stage):
        for far in (1, 0):
            send(("rs1", stage, far), part.at[:, rows_of(stage, far, 1 - core), :], rs1.at[stage, far], to_c)

    n_rs = 4
    rs_rows = hrows // n_rs

    def add_far(stage):
        arrive(("rs1", stage, 1), rs1.at[stage, 1])
        for n in range(width):
            total = part[n, rows_of(stage, 1, core), :].astype(F32) + rs1[stage, 1, n].astype(F32)
            send2[stage, n] = total.astype(BF16)

    def send_far(stage):
        for j in range(n_rs):
            where = pl.ds(j * rs_rows, rs_rows)
            send(("rs2", stage, j), send2.at[stage, :, where, :], rs2.at[stage, :, where, :], to_y)

    def finish(stage):
        arrive(("rs1", stage, 0), rs1.at[stage, 0])
        base = stage * hrows * width
        for j in range(n_rs):
            where = pl.ds(j * rs_rows, rs_rows)
            arrive(("rs2", stage, j), rs2.at[stage, :, where, :])
            yy = y
            column = 1 - x if stage == 0 else x
            start = (2 * yy + column) * rows + core * hrows + j * rs_rows
            near = pl.ds(pl.multiple_of(start, rs_rows), rs_rows)
            for n in range(width):
                total = part[n, near, :].astype(F32) + rs1[stage, 0, n, where, :].astype(F32)
                total += rs2[stage, n, where, :].astype(F32)
                for i in range(cuts):
                    acc[i, pl.ds(base + j * rs_rows * width + n, rs_rows, stride=width), :] = (
                        total[:, i * lanes:(i + 1) * lanes])
            high = pl.ds(j * rs_rows * width, rs_rows * width)
            whole = jnp.concatenate(
                [acc[i, pl.ds(base + j * rs_rows * width, rs_rows * width), :] for i in range(cuts)], axis=1)
            nl_own[stage, high, :] = whole.astype(BF16)
            nl_out[stage, where] = whole.reshape(rs_rows, width, chi).astype(BF16)
            send(("up", stage, j), nl_own.at[stage, high, :], nl_in.at[stage, high, :], to_up, when=shifts)
            keep(("up", stage, j), nl_own.at[stage, high, :], nl_in.at[stage, high, :], rests)

    my_half = pl.ds(pl.multiple_of(core * hrows, hrows), hrows)
    mate_half = pl.ds(pl.multiple_of((1 - core) * hrows, hrows), hrows)
    nl_slots = [slot(("nl_land", h)) for h in range(2)]
    assert nl_slots[1] == nl_slots[0] + 1
    nl_land = nl_slots[0] + core
    n_out = 4
    out_slots = [[slot(("out_land", h, j)) for j in range(n_out)] for h in range(2)]
    out_rows = hrows // n_out

    def home_left(stage):
        src, dst = nl_out.at[stage], new_left.at[my_half]
        if stage == 0:
            send(("nl0", 0), src, dst, to_x, when=stays, land=nl_land)
            send(("nl0", 1), src, dst, to_xc, when=moves, land=nl_land)
        else:
            send(("nl1", 0), src, dst, to_c, when=moves, land=nl_land)
            keep(("nl1", 1), src, dst, stays, land=nl_land)

    def home_product(stage, j):
        start = core * hrows + j * out_rows
        dst = product.at[pl.ds(pl.multiple_of(start, out_rows), out_rows)]
        src = prod.at[stage, pl.ds(j * out_rows, out_rows)]
        land = out_slots[0][j] + core * n_out
        if stage == 0:
            send(("out0", j, 0), src, dst, to_xc, when=stays, land=land)
            send(("out0", j, 1), src, dst, to_x, when=moves, land=land)
        else:
            send(("out1", j, 0), src, dst, to_c, when=stays, land=land)
            keep(("out1", j, 1), src, dst, moves, land=land)

    partial(0)
    swap_halves(0)
    partial(1)
    add_far(0)
    swap_halves(1)
    send_far(0)
    late(0)
    launch(3)

    side = width * pq
    col = iota((small, side), 1)
    col_m = lax.rem(col, width)
    col_sv = lax.rem(lax.div(col, width), pq // 2) * 2 + lax.div(col, width * (pq // 2))
    col_s, col_v = lax.div(col_sv, phys), lax.rem(col_sv, phys)
    row = iota((side, small), 0)
    row_k, row_u, row_w = lax.div(row, pq), lax.rem(lax.div(row, phys), phys), lax.rem(row, phys)
    code_c, code_r = iota((small, side), 0), iota((side, small), 1)
    t1 = mm(mpo[...], one_hot(col_s * width + col_m == code_c)).astype(BF16)
    t2 = mm(one_hot(row_w * width + row_k == code_r), mpo[...]).astype(BF16)
    both = jnp.zeros((side, side), F32)
    for n in range(width):
        near = mm(one_hot(row_u * width + n == code_r), t1)
        both += near * mm(t2, one_hot(col_v * width + n == code_c))
    pair[...] = both.astype(BF16)

    add_far(1)
    late(1)
    finish(0)
    home_left(0)
    relay(0)
    spread(2)
    arrive("right", right)

    def strip_of(stage, q):
        ours = nl_in[stage]

        @pl.loop(0, pq // 2)
        def _(t):
            mixed[t] = mm(ours, psi[q, t])

        @pl.loop(0, batch // 2, unroll=4)
        def _(p):
            here = mixed[:, pl.ds(pl.multiple_of(p * 2 * width, 2 * width), 2 * width), :]
            tiles = []
            for i in range(2):
                one = here[:, i * width:(i + 1) * width, :].reshape(pq // 2 * width, 2 * lanes)
                tiles.append(jnp.concatenate([one[:, :lanes], one[:, lanes:]], axis=0))
            both = jnp.concatenate(tiles, axis=1).astype(BF16)
            out = mm(pair[...], both).astype(BF16)
            for i in range(2):
                where = pl.ds(pl.multiple_of((p * 2 + i) * pq, pq), pq)
                for k in range(width):
                    piece = out[k * pq:(k + 1) * pq, i * lanes:(i + 1) * lanes]
                    proj[where, k * lanes:(k + 1) * lanes] = piece

        env = right[:, q * lanes:(q + 1) * lanes, :].reshape(width * lanes, chi)
        high = out_rows * pq
        for j in range(n_out):
            total = mm(proj[j * high:(j + 1) * high, :], env)
            long = pl.ds(stage * batch * pq + j * high, high)
            if q > 0:
                total += jnp.concatenate([acc[i, long, :] for i in range(cuts)], axis=1)
            if q < cuts - 1:
                for i in range(cuts):
                    acc[i, long, :] = total[:, i * lanes:(i + 1) * lanes]
            else:
                out = total.reshape(out_rows, phys, phys, chi).astype(BF16)
                prod[stage, j * out_rows:(j + 1) * out_rows] = out
                home_product(stage, j)

    complete(0)
    for j in range(n_rs):
        high = pl.ds(j * rs_rows * width, rs_rows * width)
        arrive(("up", 0, j), nl_in.at[0, high, :])
    strip_of(0, 0)
    relay(1)
    spread(3)
    send_far(1)
    complete(1)
    strip_of(0, 1)
    relay(2)
    complete(2)
    strip_of(0, 2)
    relay(3)
    complete(3)
    strip_of(0, 3)
    finish(1)
    home_left(1)
    for j in range(n_rs):
        high = pl.ds(j * rs_rows * width, rs_rows * width)
        arrive(("up", 1, j), nl_in.at[1, high, :])
    for q in range(cuts):
        strip_of(1, q)

    for h in range(2):
        where = pl.ds(h * hrows, hrows)
        arrive(("nl_land", h), new_left.at[where])
        for j in range(n_out):
            arrive(("out_land", h, j), product.at[pl.ds(h * hrows + j * out_rows, out_rows)])
    for copies in started.values():
        for copy, when in copies:
            if when is None:
                copy.wait_send()
            else:
                pl.when(when)(copy.wait_send)


def fused(left_env, site, psi, right_env, mpo):
    _, rows, width, chi = left_env.shape
    phys = site.shape[2]
    pq = phys * phys
    group, cuts, batch = 16, 4, rows // 2
    lanes = chi // cuts
    small = phys * width
    table = mpo.transpose(3, 1, 2, 0).reshape(small, small)
    n_sems = 120
    any_spec = pl.BlockSpec(memory_space=pl.ANY)
    vmem = pl.BlockSpec(memory_space=pltpu.VMEM)
    new_left, product = pl.pallas_call(
        functools.partial(kernel, (rows, width, phys, chi, group, cuts, batch)),
        out_shape=(
            jax.ShapeDtypeStruct((rows, width, chi), BF16),
            jax.ShapeDtypeStruct((rows, phys, phys, chi), BF16),
        ),
        in_specs=[any_spec] * 5,
        out_specs=(vmem, vmem),
        scratch_shapes=[
            pltpu.VMEM((rows, width, chi), BF16),
            pltpu.VMEM((rows, phys, chi), BF16),
            pltpu.VMEM((rows, phys, phys, chi), BF16),
            pltpu.VMEM((small, small), BF16),
            pltpu.VMEM((width, chi, chi), BF16),
            pltpu.VMEM((phys, rows, chi), BF16),
            pltpu.VMEM((cuts, pq // 2, rows, 2 * lanes), BF16),
            pltpu.VMEM((phys, chi, chi), BF16),
            pltpu.VMEM((chi, phys * rows), BF16),
            pltpu.VMEM((small * group, small * group), BF16),
            pltpu.VMEM((width * pq, width * pq), BF16),
            pltpu.VMEM((width, phys * rows, chi), BF16),
            pltpu.VMEM((width, chi, chi), BF16),
            pltpu.VMEM((2, 2, width, rows // 2, chi), BF16),
            pltpu.VMEM((2, width, rows // 2, chi), BF16),
            pltpu.VMEM((2, width, rows // 2, chi), BF16),
            pltpu.VMEM((2, rows // 2 * width, chi), BF16),
            pltpu.VMEM((2, rows // 2, width, chi), BF16),
            pltpu.VMEM((2, rows // 2 * width, chi), BF16),
            pltpu.VMEM((cuts, pq // 2, chi, 2 * lanes), BF16),
            pltpu.VMEM((pq // 2, batch * width, 2 * lanes), F32),
            pltpu.VMEM((batch * pq, width * lanes), BF16),
            pltpu.VMEM((2, rows // 2, phys, phys, chi), BF16),
            pltpu.VMEM((cuts, rows * pq, lanes), F32),
            pltpu.SemaphoreType.DMA((6,)),
            pltpu.SemaphoreType.DMA((n_sems,)),
            pltpu.SemaphoreType.DMA((n_sems,)),
        ],
        compiler_params=pltpu.CompilerParams(
            collective_id=0, has_side_effects=True, vmem_limit_bytes=62 * 1024 * 1024
        ),
    )(left_env[0], site[0], psi[0], right_env[0], table)
    return new_left[None], product[None]


def shifted(block, axis, distance):
    devices = range(lax.axis_size(axis))
    route = [((i - distance) % len(devices), i) for i in devices]
    return lax.ppermute(block, axis, route)


def shards(left_env, site, psi, right_env, mpo):
    left = left_env[0]
    tensor = site[0]
    rows = tensor.shape[0]
    phys = tensor.shape[1]
    chi = tensor.shape[2]
    width = left.shape[1]
    pair_source = shifted(psi[0], "sec", 1)
    offset = lax.axis_index("bond") * rows
    whole_left, whole_site = (
        lax.all_gather(left, "bond", axis=0, tiled=True),
        lax.all_gather(tensor, "bond", axis=0, tiled=True),
    )
    own_cols = lax.dynamic_slice_in_dim(whole_site, offset, rows, 2)
    first = jnp.dot(
        whole_left.reshape(chi * width, chi),
        own_cols.reshape(chi, phys * rows),
        preferred_element_type=jnp.float32,
    )
    first = first.astype(jnp.bfloat16).reshape(chi, width, phys, rows)
    second = jnp.einsum("pmsb,mnsu->punb", first, mpo, preferred_element_type=jnp.float32).astype(
        jnp.bfloat16
    )
    fresh = lax.dot_general(
        whole_site.reshape(chi * phys, chi),
        second.reshape(chi * phys, width * rows),
        (((0,), (0,)), ((), ())),
        preferred_element_type=jnp.float32,
    )
    fresh = fresh.astype(jnp.bfloat16).reshape(chi, width, rows)
    new_left = lax.all_to_all(fresh, "bond", split_axis=0, concat_axis=2, tiled=True)
    left_source = shifted(new_left, "sec", 1)
    source_flat = left_source.reshape(rows * width, chi)
    pair = pair_source.reshape(rows, phys * phys * chi)
    mixed = jnp.dot(
        source_flat,
        lax.all_gather(pair, "bond", axis=0, tiled=True),
        preferred_element_type=jnp.float32,
    )
    mixed = mixed.astype(jnp.bfloat16).reshape(rows, width * phys * phys, chi)
    two_site = jnp.einsum("mnsu,nkvw->msvuwk", mpo, mpo, preferred_element_type=jnp.float32)
    two_site = two_site.astype(jnp.bfloat16).reshape(width * phys * phys, phys * phys * width)
    projected = jnp.einsum(
        "pqc,qr->prc", mixed, two_site, preferred_element_type=jnp.float32
    ).astype(jnp.bfloat16)
    env_right = right_env[0].reshape(width * chi, chi)
    result = jnp.dot(
        projected.reshape(rows * phys * phys, width * chi),
        env_right,
        preferred_element_type=jnp.float32,
    ).astype(jnp.bfloat16)
    return (new_left[None], result.reshape(1, rows, phys, phys, chi))


def solution(mesh):
    in_specs = (
        P("sec", "bond", None, None),
        P("sec", "bond", None, None),
        P("sec", "bond", None, None, None),
        P("sec", None, None, None),
        P(),
    )
    out_specs = (P("sec", "bond", None, None), P("sec", "bond", None, None, None))
    body = fused if mesh.shape["bond"] == 4 else shards
    return jax.shard_map(body, mesh=mesh, in_specs=in_specs, out_specs=out_specs, check_vma=False)
```

```python
import functools

import jax
import jax.numpy as jnp
from jax import lax
from jax.experimental import pallas as pl
from jax.experimental.pallas import tpu as pltpu
from jax.sharding import PartitionSpec as P

MESH = pl.DeviceIdType.MESH
BF16 = jnp.bfloat16
F32 = jnp.float32


def mm(a, b):
    return jnp.dot(a, b, preferred_element_type=F32)


def kernel(
    dims,
    left_h, site_h, psi_h, right_h, mpo_h,
    new_left, product,
    left, site_raw, psi_raw, mpo, right,
    site_own, psi_own, site, site_tr, mix, pair,
    second, part, rs1, send2, rs2, nl_own, nl_out, nl_in, psi, mixed, proj, prod, acc,
    local_sem, send_sem, recv_sem,
):
    rows, width, phys, chi, group, cuts, batch = dims
    pq = phys * phys
    n_sec = lax.axis_size("sec")
    sec = lax.axis_index("sec")
    me = lax.axis_index("bond")
    x, y = lax.rem(me, 2), me // 2
    core, z = lax.rem(sec, 2), sec // 2
    mate_sec = 2 * z + 1 - core
    side_bond = 2 * y + 1 - x
    to_c = {"sec": mate_sec}
    to_y = {"bond": 2 * (1 - y) + x}
    to_x = {"bond": side_bond}
    to_xc = {"sec": mate_sec, "bond": side_bond}
    up = lax.rem(sec + 2, n_sec)
    to_up = {"sec": up}
    stays = x == core
    moves = x != core
    shifts = x == 1
    rests = x == 0

    mine = 2 * y + core
    mates = 2 * y + 1 - core
    across = 2 * (1 - y) + core
    corner = 2 * (1 - y) + 1 - core

    def block(owner):
        return pl.ds(pl.multiple_of(owner * rows, rows), rows)

    loads = {}
    for i, (name, src, dst) in enumerate((
        ("site", site_h, site_raw),
        ("psi", psi_h, psi_raw),
        ("mpo", mpo_h, mpo),
    )):
        loads[name] = pltpu.make_async_copy(src, dst, local_sem.at[i])
        loads[name].start()

    barrier = pltpu.get_barrier_semaphore()
    greeted = [to_c, to_y, to_x, to_xc]
    for dz in (2, n_sec - 2):
        greeted.append({"sec": lax.rem(sec + dz, n_sec)})
        greeted.append({"sec": lax.rem(mate_sec + dz, n_sec), "bond": side_bond})
    for target in greeted:
        pl.semaphore_signal(barrier, inc=1, device_id=target, device_id_type=MESH)
    pl.semaphore_wait(barrier, len(greeted))

    started = {}
    counter = {}
    lands = {}
    landed = set()

    def slot(key):
        return counter.setdefault(key, len(counter))

    def remote(i, j, src, dst, target):
        return pltpu.make_async_remote_copy(
            src_ref=src, dst_ref=dst, send_sem=send_sem.at[i], recv_sem=recv_sem.at[j],
            device_id=target, device_id_type=MESH,
        )

    def send(key, src, dst, target, when=None, land=None):
        i = slot(key)
        copy = remote(i, i if land is None else land, src, dst, target)
        if when is None:
            copy.start()
        else:
            pl.when(when)(copy.start)
        started.setdefault(key, []).append((copy, when))
        lands[key] = dst

    def keep(key, src, dst, when, land=None):
        copy = pltpu.make_async_copy(src, dst, recv_sem.at[slot(key) if land is None else land])
        pl.when(when)(copy.start)

    def arrive(key, dst):
        i = slot(key)
        landed.add(key)
        remote(i, i, dst, dst, to_c).wait_recv()

    lanes = chi // cuts
    pieces = tuple(pl.ds(t, 1) for t in range(phys))
    n_left = 4
    tall_left = rows // n_left

    def left_part(i):
        return pl.ds(i * tall_left, tall_left)

    def send_left(i):
        send(("left", i), left_h.at[left_part(i)], left.at[left_part(i)], to_xc, when=moves)
        keep(("left", i), left_h.at[left_part(i)], left.at[left_part(i)], stays)

    loads["site"].wait()
    flat = site_raw[...].astype(F32).reshape(rows * phys, chi)
    for i in range(cuts):
        acc[i, :rows * phys, :] = flat[:, i * lanes:(i + 1) * lanes]
    for t in range(phys):
        for i in range(cuts):
            tile = acc[i, pl.ds(t, rows, stride=phys), :]
            site_own[t, :, i * lanes:(i + 1) * lanes] = tile.astype(BF16)

    def site_spread(p, from_own):
        src = site_own.at[pieces[p]] if from_own else site.at[pieces[p], block(mine), :]
        when = stays if from_own else None
        send(("site_y", p), src, site.at[pieces[p], block(mine), :], to_y, when)
        send(("site_c", p), src, site.at[pieces[p], block(mine), :], to_c, when)

    for p in range(phys):
        send(("site", p), site_own.at[pieces[p]], site.at[pieces[p], block(me), :], to_xc, when=moves)
        keep(("site", p), site_own.at[pieces[p]], site.at[pieces[p], block(me), :], stays)
        site_spread(p, True)
    for i in range(n_left):
        send_left(i)

    loads["psi"].wait()
    tall = 8

    @pl.loop(0, rows // tall)
    def _(g):
        flat = psi_raw[pl.ds(pl.multiple_of(g * tall, tall), tall)].astype(F32)
        flat = flat.reshape(tall * pq, chi)
        where = pl.ds(pl.multiple_of(g * tall * pq, tall * pq), tall * pq)
        for i in range(cuts):
            acc[i, where, :] = flat[:, i * lanes:(i + 1) * lanes]

    def region(q, owner):
        return psi.at[q, :, block(owner), :]

    psi_self = jnp.logical_and(x == 0, core == 0)
    to_psi = {
        "sec": lax.rem(2 * z + x + 2 * core, n_sec),
        "bond": 2 * y + core,
    }

    psi_waits = jnp.logical_and(x == 0, core == 1)
    psi_now = x == 1

    def launch(q):
        send(("own", q), psi_own.at[q], region(q, me), to_psi, when=psi_now)
        keep(("own", q), psi_own.at[q], region(q, me), psi_self)

    def launch_late(q):
        send(("own", q), psi_own.at[q], region(q, me), to_psi, when=psi_waits)

    for q in range(cuts):
        for t in range(pq):
            at = (t % 2) * lanes
            tile = acc[q, pl.ds(t, rows, stride=pq), :]
            psi_own[q, t // 2, :, at:at + lanes] = tile.astype(BF16)
        if q > 0:
            launch(q - 1)
    launch(cuts - 1)

    def spread_if(q, when, last):
        @pl.when(when)
        def _():
            arrive(("own", q), region(q, mine))
            for key, target in (("psi_y", to_y), ("psi_c", to_c)):
                i = slot((key, q))
                remote(i, i, region(q, mine), region(q, mine), target).start()
        if last:
            for key, target in (("psi_y", to_y), ("psi_c", to_c)):
                i = slot((key, q))
                started[(key, q)] = [(remote(i, i, region(q, mine), region(q, mine), target), None)]
                lands[(key, q)] = region(q, mine)

    stays_up = jnp.logical_and(x == 1, core == 1)

    def relay(q):
        arrive(("psi_y", q), region(q, across))
        send(("psi_yc", q), region(q, across), region(q, across), to_c)

    def complete(q):
        arrive(("psi_c", q), region(q, mates))
        arrive(("psi_yc", q), region(q, corner))

    spread_if(0, psi_self, False)
    spread_if(1, psi_self, False)

    @pl.when(moves)
    def _():
        for p in range(phys):
            arrive(("site", p), site.at[pieces[p], block(mine), :])
            src = site.at[pieces[p], block(mine), :]
            remote(slot(("site_y", p)), slot(("site_y", p)), src, src, to_y).start()
            remote(slot(("site_c", p)), slot(("site_c", p)), src, src, to_c).start()

    @pl.when(stays)
    def _():
        for p in range(phys):
            arrive(("site", p), site.at[pieces[p], block(mine), :])

    for p in range(phys):
        for key, target in (("site_y", to_y), ("site_c", to_c)):
            src = site.at[pieces[p], block(mine), :]
            i = slot((key, p))
            started[(key, p)] = [(remote(i, i, src, src, target), None)]

    loads["mpo"].wait()

    def iota(shape, axis):
        return lax.broadcasted_iota(jnp.int32, shape, axis)

    def one_hot(condition):
        return jnp.where(condition, 1.0, 0.0).astype(BF16)

    small = phys * width
    big = small * group
    tall_code = lax.div(iota((big, small), 0), group)
    spread_rows = one_hot(tall_code == iota((big, small), 1))
    col = iota((small, big), 1)
    col_code = lax.div(col, group * width) * width + lax.rem(col, width)
    spread_cols = one_hot(col_code == iota((small, big), 0))
    wide = mm(mm(spread_rows, mpo[...]).astype(BF16), spread_cols)
    same = lax.rem(iota((big, big), 0), group) == lax.rem(lax.div(iota((big, big), 1), width), group)
    mix[...] = jnp.where(same, wide, 0.0).astype(BF16)

    for t in range(phys):
        own = site[t, block(mine), :].astype(F32)
        for i in range(cuts):
            tile = own[:, i * lanes:(i + 1) * lanes]
            site_tr[i * lanes:(i + 1) * lanes, t * rows:(t + 1) * rows] = tile.T.astype(BF16)

    for p in range(phys):
        arrive(("site_y", p), site.at[pieces[p], block(across), :])
        send(("site_yc", p), site.at[pieces[p], block(across), :], site.at[pieces[p], block(across), :], to_c)

    spread_if(0, stays_up, False)
    for p in range(phys):
        arrive(("site_c", p), site.at[pieces[p], block(mates), :])
        arrive(("site_yc", p), site.at[pieces[p], block(corner), :])

    send(("right",), right_h, right, to_c, when=moves)
    keep(("right",), right_h, right, moves)
    strip = group * width
    per_left = tall_left // group

    for i in range(n_left):
        arrive(("left", i), left.at[left_part(i)])

        @pl.loop(i * per_left, (i + 1) * per_left)
        def _(g):
            ours = left[pl.ds(pl.multiple_of(g * group, group), group)].astype(F32)
            ours = ours.reshape(strip, chi).astype(BF16)
            first = jnp.concatenate([mm(ours, site[s]).astype(BF16) for s in range(phys)], axis=0)
            out = mm(mix[...], first).astype(BF16)
            for u in range(phys):
                for n in range(width):
                    at = (u * width + n) * group
                    where = pl.multiple_of(u * rows + g * group, group)
                    second[n, pl.ds(where, group), :] = out[at:at + group, :]

        if i == 0:
            spread_if(1, stays_up, False)
        if i == n_left - 2:
            for q in range(cuts):
                launch_late(q)


    hrows = rows // 2

    def rows_of(stage, far, half):
        yy = 1 - y if far else y
        column = 1 - x if stage == 0 else x
        start = (2 * yy + column) * rows + half * hrows
        return pl.ds(pl.multiple_of(start, hrows), hrows)

    def block_of(stage, far):
        yy = 1 - y if far else y
        column = 1 - x if stage == 0 else x
        return block(2 * yy + column)

    def partial(stage):
        for far in (1, 0):
            where = block_of(stage, far)
            for n in range(width):
                part[n, where, :] = mm(site_tr[where, :], second[n]).astype(BF16)

    def swap_halves(stage):
        for far in (1, 0):
            send(("rs1", stage, far), part.at[:, rows_of(stage, far, 1 - core), :], rs1.at[stage, far], to_c)

    n_rs = 4
    rs_rows = hrows // n_rs

    def add_far(stage):
        arrive(("rs1", stage, 1), rs1.at[stage, 1])
        for n in range(width):
            total = part[n, rows_of(stage, 1, core), :].astype(F32) + rs1[stage, 1, n].astype(F32)
            send2[stage, n] = total.astype(BF16)

    def send_far(stage):
        for j in range(n_rs):
            where = pl.ds(j * rs_rows, rs_rows)
            send(("rs2", stage, j), send2.at[stage, :, where, :], rs2.at[stage, :, where, :], to_y)

    def finish(stage):
        arrive(("rs1", stage, 0), rs1.at[stage, 0])
        base = stage * hrows * width
        for j in range(n_rs):
            where = pl.ds(j * rs_rows, rs_rows)
            arrive(("rs2", stage, j), rs2.at[stage, :, where, :])
            yy = y
            column = 1 - x if stage == 0 else x
            start = (2 * yy + column) * rows + core * hrows + j * rs_rows
            near = pl.ds(pl.multiple_of(start, rs_rows), rs_rows)
            for n in range(width):
                total = part[n, near, :].astype(F32) + rs1[stage, 0, n, where, :].astype(F32)
                total += rs2[stage, n, where, :].astype(F32)
                for i in range(cuts):
                    acc[i, pl.ds(base + j * rs_rows * width + n, rs_rows, stride=width), :] = (
                        total[:, i * lanes:(i + 1) * lanes])
            high = pl.ds(j * rs_rows * width, rs_rows * width)
            whole = jnp.concatenate(
                [acc[i, pl.ds(base + j * rs_rows * width, rs_rows * width), :] for i in range(cuts)], axis=1)
            nl_own[stage, high, :] = whole.astype(BF16)
            nl_out[stage, where] = whole.reshape(rs_rows, width, chi).astype(BF16)
            send(("up", stage, j), nl_own.at[stage, high, :], nl_in.at[stage, high, :], to_up, when=shifts)
            keep(("up", stage, j), nl_own.at[stage, high, :], nl_in.at[stage, high, :], rests)

    my_half = pl.ds(pl.multiple_of(core * hrows, hrows), hrows)
    mate_half = pl.ds(pl.multiple_of((1 - core) * hrows, hrows), hrows)
    nl_slots = [slot(("nl_land", h)) for h in range(2)]
    assert nl_slots[1] == nl_slots[0] + 1
    nl_land = nl_slots[0] + core
    n_out = 4
    out_slots = [[slot(("out_land", h, j)) for j in range(n_out)] for h in range(2)]
    out_rows = hrows // n_out

    def home_left(stage):
        src, dst = nl_out.at[stage], new_left.at[my_half]
        if stage == 0:
            send(("nl0", 0), src, dst, to_x, when=stays, land=nl_land)
            send(("nl0", 1), src, dst, to_xc, when=moves, land=nl_land)
        else:
            send(("nl1", 0), src, dst, to_c, when=moves, land=nl_land)
            keep(("nl1", 1), src, dst, stays, land=nl_land)

    def home_product(stage, j):
        start = core * hrows + j * out_rows
        dst = product.at[pl.ds(pl.multiple_of(start, out_rows), out_rows)]
        src = prod.at[stage, pl.ds(j * out_rows, out_rows)]
        land = out_slots[0][j] + core * n_out
        if stage == 0:
            send(("out0", j, 0), src, dst, to_xc, when=stays, land=land)
            send(("out0", j, 1), src, dst, to_x, when=moves, land=land)
        else:
            send(("out1", j, 0), src, dst, to_c, when=stays, land=land)
            keep(("out1", j, 1), src, dst, moves, land=land)

    def finalize():
        for key in list(started):
            if key[0] not in ("nl0", "nl1", "out0", "out1") and key not in landed:
                arrive(key, lands[key])
        for h in range(2):
            where = pl.ds(h * hrows, hrows)
            for stage, when in ((0, moves), (1, stays)):
                if (f"nl{stage}", 0) in started:
                    pl.when(when)(functools.partial(arrive, ("nl_land", h), new_left.at[where]))
            for stage, when in ((0, stays), (1, moves)):
                for j in range(n_out):
                    if (f"out{stage}", j, 0) in started:
                        where = pl.ds(h * hrows + j * out_rows, out_rows)
                        pl.when(when)(functools.partial(arrive, ("out_land", h, j), product.at[where]))
        for copies in started.values():
            for copy, when in copies:
                if when is None:
                    copy.wait_send()
                else:
                    pl.when(when)(copy.wait_send)

    partial(0)
    swap_halves(0)
    partial(1)
    add_far(0)
    swap_halves(1)
    send_far(0)
    spread_if(2, stays, False)
    spread_if(0, moves, True)

    side = width * pq
    col = iota((small, side), 1)
    col_m = lax.rem(col, width)
    col_sv = lax.rem(lax.div(col, width), pq // 2) * 2 + lax.div(col, width * (pq // 2))
    col_s, col_v = lax.div(col_sv, phys), lax.rem(col_sv, phys)
    row = iota((side, small), 0)
    row_k, row_u, row_w = lax.div(row, pq), lax.rem(lax.div(row, phys), phys), lax.rem(row, phys)
    code_c, code_r = iota((small, side), 0), iota((side, small), 1)
    t1 = mm(mpo[...], one_hot(col_s * width + col_m == code_c)).astype(BF16)
    t2 = mm(one_hot(row_w * width + row_k == code_r), mpo[...]).astype(BF16)
    both = jnp.zeros((side, side), F32)
    for n in range(width):
        near = mm(one_hot(row_u * width + n == code_r), t1)
        both += near * mm(t2, one_hot(col_v * width + n == code_c))
    pair[...] = both.astype(BF16)

    add_far(1)
    spread_if(1, moves, True)
    finish(0)
    home_left(0)
    spread_if(2, moves, True)
    spread_if(3, stays, False)
    relay(0)
    arrive(("right",), right)

    def strip_of(stage, q):
        ours = nl_in[stage]

        @pl.loop(0, pq // 2)
        def _(t):
            mixed[t] = mm(ours, psi[q, t])

        @pl.loop(0, batch // 2, unroll=4)
        def _(p):
            here = mixed[:, pl.ds(pl.multiple_of(p * 2 * width, 2 * width), 2 * width), :]
            tiles = []
            for i in range(2):
                one = here[:, i * width:(i + 1) * width, :].reshape(pq // 2 * width, 2 * lanes)
                tiles.append(jnp.concatenate([one[:, :lanes], one[:, lanes:]], axis=0))
            both = jnp.concatenate(tiles, axis=1).astype(BF16)
            out = mm(pair[...], both).astype(BF16)
            for i in range(2):
                where = pl.ds(pl.multiple_of((p * 2 + i) * pq, pq), pq)
                for k in range(width):
                    piece = out[k * pq:(k + 1) * pq, i * lanes:(i + 1) * lanes]
                    proj[where, k * lanes:(k + 1) * lanes] = piece

        env = right[:, q * lanes:(q + 1) * lanes, :].reshape(width * lanes, chi)
        high = out_rows * pq
        for j in range(n_out):
            total = mm(proj[j * high:(j + 1) * high, :], env)
            long = pl.ds(stage * batch * pq + j * high, high)
            if q > 0:
                total += jnp.concatenate([acc[i, long, :] for i in range(cuts)], axis=1)
            if q < cuts - 1:
                for i in range(cuts):
                    acc[i, long, :] = total[:, i * lanes:(i + 1) * lanes]
            else:
                out = total.reshape(out_rows, phys, phys, chi).astype(BF16)
                prod[stage, j * out_rows:(j + 1) * out_rows] = out
                home_product(stage, j)

    complete(0)
    for j in range(n_rs):
        high = pl.ds(j * rs_rows * width, rs_rows * width)
        arrive(("up", 0, j), nl_in.at[0, high, :])
    strip_of(0, 0)
    relay(1)
    spread_if(3, moves, True)
    complete(1)
    strip_of(0, 1)
    relay(2)
    complete(2)
    strip_of(0, 2)
    send_far(1)
    relay(3)
    complete(3)
    strip_of(0, 3)
    finish(1)
    home_left(1)
    for j in range(n_rs):
        high = pl.ds(j * rs_rows * width, rs_rows * width)
        arrive(("up", 1, j), nl_in.at[1, high, :])
    for q in range(cuts):
        strip_of(1, q)

    finalize()


def fused(left_env, site, psi, right_env, mpo):
    _, rows, width, chi = left_env.shape
    phys = site.shape[2]
    pq = phys * phys
    group, cuts, batch = 16, 4, rows // 2
    lanes = chi // cuts
    small = phys * width
    table = mpo.transpose(3, 1, 2, 0).reshape(small, small)
    n_sems = 120
    any_spec = pl.BlockSpec(memory_space=pl.ANY)
    vmem = pl.BlockSpec(memory_space=pltpu.VMEM)
    new_left, product = pl.pallas_call(
        functools.partial(kernel, (rows, width, phys, chi, group, cuts, batch)),
        out_shape=(
            jax.ShapeDtypeStruct((rows, width, chi), BF16),
            jax.ShapeDtypeStruct((rows, phys, phys, chi), BF16),
        ),
        in_specs=[any_spec] * 5,
        out_specs=(vmem, vmem),
        scratch_shapes=[
            pltpu.VMEM((rows, width, chi), BF16),
            pltpu.VMEM((rows, phys, chi), BF16),
            pltpu.VMEM((rows, phys, phys, chi), BF16),
            pltpu.VMEM((small, small), BF16),
            pltpu.VMEM((width, chi, chi), BF16),
            pltpu.VMEM((phys, rows, chi), BF16),
            pltpu.VMEM((cuts, pq // 2, rows, 2 * lanes), BF16),
            pltpu.VMEM((phys, chi, chi), BF16),
            pltpu.VMEM((chi, phys * rows), BF16),
            pltpu.VMEM((small * group, small * group), BF16),
            pltpu.VMEM((width * pq, width * pq), BF16),
            pltpu.VMEM((width, phys * rows, chi), BF16),
            pltpu.VMEM((width, chi, chi), BF16),
            pltpu.VMEM((2, 2, width, rows // 2, chi), BF16),
            pltpu.VMEM((2, width, rows // 2, chi), BF16),
            pltpu.VMEM((2, width, rows // 2, chi), BF16),
            pltpu.VMEM((2, rows // 2 * width, chi), BF16),
            pltpu.VMEM((2, rows // 2, width, chi), BF16),
            pltpu.VMEM((2, rows // 2 * width, chi), BF16),
            pltpu.VMEM((cuts, pq // 2, chi, 2 * lanes), BF16),
            pltpu.VMEM((pq // 2, batch * width, 2 * lanes), F32),
            pltpu.VMEM((batch * pq, width * lanes), BF16),
            pltpu.VMEM((2, rows // 2, phys, phys, chi), BF16),
            pltpu.VMEM((cuts, rows * pq, lanes), F32),
            pltpu.SemaphoreType.DMA((6,)),
            pltpu.SemaphoreType.DMA((n_sems,)),
            pltpu.SemaphoreType.DMA((n_sems,)),
        ],
        compiler_params=pltpu.CompilerParams(
            collective_id=0, has_side_effects=True, vmem_limit_bytes=62 * 1024 * 1024
        ),
    )(left_env[0], site[0], psi[0], right_env[0], table)
    return new_left[None], product[None]


def shifted(block, axis, distance):
    devices = range(lax.axis_size(axis))
    route = [((i - distance) % len(devices), i) for i in devices]
    return lax.ppermute(block, axis, route)


def shards(left_env, site, psi, right_env, mpo):
    left = left_env[0]
    tensor = site[0]
    rows = tensor.shape[0]
    phys = tensor.shape[1]
    chi = tensor.shape[2]
    width = left.shape[1]
    pair_source = shifted(psi[0], "sec", 1)
    offset = lax.axis_index("bond") * rows
    whole_left, whole_site = (
        lax.all_gather(left, "bond", axis=0, tiled=True),
        lax.all_gather(tensor, "bond", axis=0, tiled=True),
    )
    own_cols = lax.dynamic_slice_in_dim(whole_site, offset, rows, 2)
    first = jnp.dot(
        whole_left.reshape(chi * width, chi),
        own_cols.reshape(chi, phys * rows),
        preferred_element_type=jnp.float32,
    )
    first = first.astype(jnp.bfloat16).reshape(chi, width, phys, rows)
    second = jnp.einsum("pmsb,mnsu->punb", first, mpo, preferred_element_type=jnp.float32).astype(
        jnp.bfloat16
    )
    fresh = lax.dot_general(
        whole_site.reshape(chi * phys, chi),
        second.reshape(chi * phys, width * rows),
        (((0,), (0,)), ((), ())),
        preferred_element_type=jnp.float32,
    )
    fresh = fresh.astype(jnp.bfloat16).reshape(chi, width, rows)
    new_left = lax.all_to_all(fresh, "bond", split_axis=0, concat_axis=2, tiled=True)
    left_source = shifted(new_left, "sec", 1)
    source_flat = left_source.reshape(rows * width, chi)
    pair = pair_source.reshape(rows, phys * phys * chi)
    mixed = jnp.dot(
        source_flat,
        lax.all_gather(pair, "bond", axis=0, tiled=True),
        preferred_element_type=jnp.float32,
    )
    mixed = mixed.astype(jnp.bfloat16).reshape(rows, width * phys * phys, chi)
    two_site = jnp.einsum("mnsu,nkvw->msvuwk", mpo, mpo, preferred_element_type=jnp.float32)
    two_site = two_site.astype(jnp.bfloat16).reshape(width * phys * phys, phys * phys * width)
    projected = jnp.einsum(
        "pqc,qr->prc", mixed, two_site, preferred_element_type=jnp.float32
    ).astype(jnp.bfloat16)
    env_right = right_env[0].reshape(width * chi, chi)
    result = jnp.dot(
        projected.reshape(rows * phys * phys, width * chi),
        env_right,
        preferred_element_type=jnp.float32,
    ).astype(jnp.bfloat16)
    return (new_left[None], result.reshape(1, rows, phys, phys, chi))


def solution(mesh):
    in_specs = (
        P("sec", "bond", None, None),
        P("sec", "bond", None, None),
        P("sec", "bond", None, None, None),
        P("sec", None, None, None),
        P(),
    )
    out_specs = (P("sec", "bond", None, None), P("sec", "bond", None, None, None))
    body = fused if mesh.shape["bond"] == 4 else shards
    return jax.shard_map(body, mesh=mesh, in_specs=in_specs, out_specs=out_specs, check_vma=False)
```

```python
import functools

import jax
import jax.numpy as jnp
from jax import lax
from jax.experimental import pallas as pl
from jax.experimental.pallas import tpu as pltpu
from jax.sharding import PartitionSpec as P

MESH = pl.DeviceIdType.MESH
BF16 = jnp.bfloat16
F32 = jnp.float32


def mm(a, b):
    return jnp.dot(a, b, preferred_element_type=F32)


def kernel(
    dims,
    left_h, site_h, psi_h, right_h, mpo_h,
    new_left, product,
    left, site_raw, psi_raw, mpo, right,
    site_own, psi_own, site, site_tr, mix, pair,
    second, part, rs1, send2, rs2, nl_own, nl_out, nl_in, psi, mixed, proj, prod, acc,
    local_sem, send_sem, recv_sem,
):
    rows, width, phys, chi, group, cuts, batch = dims
    pq = phys * phys
    n_sec = lax.axis_size("sec")
    sec = lax.axis_index("sec")
    me = lax.axis_index("bond")
    x, y = lax.rem(me, 2), me // 2
    core, z = lax.rem(sec, 2), sec // 2
    mate_sec = 2 * z + 1 - core
    side_bond = 2 * y + 1 - x
    to_c = {"sec": mate_sec}
    to_y = {"bond": 2 * (1 - y) + x}
    to_x = {"bond": side_bond}
    to_xc = {"sec": mate_sec, "bond": side_bond}
    up = lax.rem(sec + 2, n_sec)
    to_up = {"sec": up}
    stays = x == core
    moves = x != core
    shifts = x == 1
    rests = x == 0

    mine = 2 * y + core
    mates = 2 * y + 1 - core
    across = 2 * (1 - y) + core
    corner = 2 * (1 - y) + 1 - core

    def block(owner):
        return pl.ds(pl.multiple_of(owner * rows, rows), rows)

    loads = {}
    for i, (name, src, dst) in enumerate((
        ("site", site_h, site_raw),
        ("psi", psi_h, psi_raw),
        ("mpo", mpo_h, mpo),
    )):
        loads[name] = pltpu.make_async_copy(src, dst, local_sem.at[i])
        loads[name].start()

    barrier = pltpu.get_barrier_semaphore()
    greeted = [to_c, to_y, to_x, to_xc]
    for dz in (2, n_sec - 2):
        greeted.append({"sec": lax.rem(sec + dz, n_sec)})
        greeted.append({"sec": lax.rem(mate_sec + dz, n_sec), "bond": side_bond})
    for target in greeted:
        pl.semaphore_signal(barrier, inc=1, device_id=target, device_id_type=MESH)
    pl.semaphore_wait(barrier, len(greeted))

    started = {}
    counter = {}
    lands = {}
    landed = set()

    def slot(key):
        return counter.setdefault(key, len(counter))

    def remote(i, j, src, dst, target):
        return pltpu.make_async_remote_copy(
            src_ref=src, dst_ref=dst, send_sem=send_sem.at[i], recv_sem=recv_sem.at[j],
            device_id=target, device_id_type=MESH,
        )

    def send(key, src, dst, target, when=None, land=None):
        i = slot(key)
        copy = remote(i, i if land is None else land, src, dst, target)
        if when is None:
            copy.start()
        else:
            pl.when(when)(copy.start)
        started.setdefault(key, []).append((copy, when))
        lands[key] = dst

    def keep(key, src, dst, when, land=None):
        copy = pltpu.make_async_copy(src, dst, recv_sem.at[slot(key) if land is None else land])
        pl.when(when)(copy.start)

    def arrive(key, dst):
        i = slot(key)
        landed.add(key)
        remote(i, i, dst, dst, to_c).wait_recv()

    lanes = chi // cuts
    pieces = tuple(pl.ds(t, 1) for t in range(phys))
    n_left = 4
    tall_left = rows // n_left

    def left_part(i):
        return pl.ds(i * tall_left, tall_left)

    def send_left(i):
        send(("left", i), left_h.at[left_part(i)], left.at[left_part(i)], to_xc, when=moves)
        keep(("left", i), left_h.at[left_part(i)], left.at[left_part(i)], stays)

    loads["site"].wait()
    flat = site_raw[...].astype(F32).reshape(rows * phys, chi)
    for i in range(cuts):
        acc[i, :rows * phys, :] = flat[:, i * lanes:(i + 1) * lanes]
    for t in range(phys):
        for i in range(cuts):
            tile = acc[i, pl.ds(t, rows, stride=phys), :]
            site_own[t, :, i * lanes:(i + 1) * lanes] = tile.astype(BF16)

    def site_spread(p, from_own):
        src = site_own.at[pieces[p]] if from_own else site.at[pieces[p], block(mine), :]
        when = stays if from_own else None
        send(("site_y", p), src, site.at[pieces[p], block(mine), :], to_y, when)
        send(("site_c", p), src, site.at[pieces[p], block(mine), :], to_c, when)

    for p in range(phys):
        send(("site", p), site_own.at[pieces[p]], site.at[pieces[p], block(me), :], to_xc, when=moves)
        keep(("site", p), site_own.at[pieces[p]], site.at[pieces[p], block(me), :], stays)
        site_spread(p, True)
    for i in range(n_left):
        send_left(i)

    loads["psi"].wait()
    tall = 8

    @pl.loop(0, rows // tall)
    def _(g):
        flat = psi_raw[pl.ds(pl.multiple_of(g * tall, tall), tall)].astype(F32)
        flat = flat.reshape(tall * pq, chi)
        where = pl.ds(pl.multiple_of(g * tall * pq, tall * pq), tall * pq)
        for i in range(cuts):
            acc[i, where, :] = flat[:, i * lanes:(i + 1) * lanes]

    def region(q, owner):
        return psi.at[q, :, block(owner), :]

    psi_self = jnp.logical_and(x == 0, core == 0)
    to_psi = {
        "sec": lax.rem(2 * z + x + 2 * core, n_sec),
        "bond": 2 * y + core,
    }

    psi_waits = jnp.logical_and(x == 0, core == 1)
    psi_now = x == 1

    def launch(q):
        send(("own", q), psi_own.at[q], region(q, me), to_psi, when=psi_now)
        keep(("own", q), psi_own.at[q], region(q, me), psi_self)

    def launch_late(q):
        send(("own", q), psi_own.at[q], region(q, me), to_psi, when=psi_waits)

    for q in range(cuts):
        for t in range(pq):
            at = (t % 2) * lanes
            tile = acc[q, pl.ds(t, rows, stride=pq), :]
            psi_own[q, t // 2, :, at:at + lanes] = tile.astype(BF16)
        if q > 0:
            launch(q - 1)
    launch(cuts - 1)

    def spread_if(q, when, last):
        @pl.when(when)
        def _():
            arrive(("own", q), region(q, mine))
            for key, target in (("psi_y", to_y), ("psi_c", to_c)):
                i = slot((key, q))
                remote(i, i, region(q, mine), region(q, mine), target).start()
        if last:
            spread_reg(q)

    def spread_reg(q):
        if True:
            for key, target in (("psi_y", to_y), ("psi_c", to_c)):
                i = slot((key, q))
                started[(key, q)] = [(remote(i, i, region(q, mine), region(q, mine), target), None)]
                lands[(key, q)] = region(q, mine)

    def relay(q):
        arrive(("psi_y", q), region(q, across))
        send(("psi_yc", q), region(q, across), region(q, across), to_c)

    def complete(q):
        arrive(("psi_c", q), region(q, mates))
        arrive(("psi_yc", q), region(q, corner))


    @pl.when(moves)
    def _():
        for p in range(phys):
            arrive(("site", p), site.at[pieces[p], block(mine), :])
            src = site.at[pieces[p], block(mine), :]
            remote(slot(("site_y", p)), slot(("site_y", p)), src, src, to_y).start()
            remote(slot(("site_c", p)), slot(("site_c", p)), src, src, to_c).start()

    @pl.when(stays)
    def _():
        for p in range(phys):
            arrive(("site", p), site.at[pieces[p], block(mine), :])

    for p in range(phys):
        for key, target in (("site_y", to_y), ("site_c", to_c)):
            src = site.at[pieces[p], block(mine), :]
            i = slot((key, p))
            started[(key, p)] = [(remote(i, i, src, src, target), None)]

    loads["mpo"].wait()

    def iota(shape, axis):
        return lax.broadcasted_iota(jnp.int32, shape, axis)

    def one_hot(condition):
        return jnp.where(condition, 1.0, 0.0).astype(BF16)

    small = phys * width
    big = small * group
    tall_code = lax.div(iota((big, small), 0), group)
    spread_rows = one_hot(tall_code == iota((big, small), 1))
    col = iota((small, big), 1)
    col_code = lax.div(col, group * width) * width + lax.rem(col, width)
    spread_cols = one_hot(col_code == iota((small, big), 0))
    wide = mm(mm(spread_rows, mpo[...]).astype(BF16), spread_cols)
    same = lax.rem(iota((big, big), 0), group) == lax.rem(lax.div(iota((big, big), 1), width), group)
    mix[...] = jnp.where(same, wide, 0.0).astype(BF16)

    for t in range(phys):
        own = site[t, block(mine), :].astype(F32)
        for i in range(cuts):
            tile = own[:, i * lanes:(i + 1) * lanes]
            site_tr[i * lanes:(i + 1) * lanes, t * rows:(t + 1) * rows] = tile.T.astype(BF16)

    for p in range(phys):
        arrive(("site_y", p), site.at[pieces[p], block(across), :])
        send(("site_yc", p), site.at[pieces[p], block(across), :], site.at[pieces[p], block(across), :], to_c)

    spread_if(0, stays, False)
    for p in range(phys):
        arrive(("site_c", p), site.at[pieces[p], block(mates), :])
        arrive(("site_yc", p), site.at[pieces[p], block(corner), :])

    send(("right",), right_h, right, to_c, when=moves)
    keep(("right",), right_h, right, moves)
    strip = group * width
    per_left = tall_left // group

    for i in range(n_left):
        arrive(("left", i), left.at[left_part(i)])

        @pl.loop(i * per_left, (i + 1) * per_left, unroll=per_left)
        def _(g):
            ours = left[pl.ds(pl.multiple_of(g * group, group), group)].astype(F32)
            ours = ours.reshape(strip, chi).astype(BF16)
            first = jnp.concatenate([mm(ours, site[s]).astype(BF16) for s in range(phys)], axis=0)
            out = mm(mix[...], first).astype(BF16)
            for u in range(phys):
                for n in range(width):
                    at = (u * width + n) * group
                    where = pl.multiple_of(u * rows + g * group, group)
                    second[n, pl.ds(where, group), :] = out[at:at + group, :]

        if i == 0:
            spread_if(1, stays, False)
        if i == n_left - 2:
            for q in range(cuts):
                launch_late(q)


    hrows = rows // 2

    def rows_of(stage, far, half):
        yy = 1 - y if far else y
        column = 1 - x if stage == 0 else x
        start = (2 * yy + column) * rows + half * hrows
        return pl.ds(pl.multiple_of(start, hrows), hrows)

    def block_of(stage, far):
        yy = 1 - y if far else y
        column = 1 - x if stage == 0 else x
        return block(2 * yy + column)

    def partial(stage):
        for far in (1, 0):
            where = block_of(stage, far)
            for n in range(width):
                part[n, where, :] = mm(site_tr[where, :], second[n]).astype(BF16)

    def swap_halves(stage):
        for far in (1, 0):
            send(("rs1", stage, far), part.at[:, rows_of(stage, far, 1 - core), :], rs1.at[stage, far], to_c)

    n_rs = 4
    rs_rows = hrows // n_rs

    def add_far(stage):
        arrive(("rs1", stage, 1), rs1.at[stage, 1])
        for n in range(width):
            total = part[n, rows_of(stage, 1, core), :].astype(F32) + rs1[stage, 1, n].astype(F32)
            send2[stage, n] = total.astype(BF16)

    def send_far(stage, when=None):
        for j in range(n_rs):
            where = pl.ds(j * rs_rows, rs_rows)
            send(("rs2", stage, j), send2.at[stage, :, where, :], rs2.at[stage, :, where, :], to_y, when=when)

    def finish(stage):
        arrive(("rs1", stage, 0), rs1.at[stage, 0])
        base = stage * hrows * width
        for j in range(n_rs):
            where = pl.ds(j * rs_rows, rs_rows)
            arrive(("rs2", stage, j), rs2.at[stage, :, where, :])
            yy = y
            column = 1 - x if stage == 0 else x
            start = (2 * yy + column) * rows + core * hrows + j * rs_rows
            near = pl.ds(pl.multiple_of(start, rs_rows), rs_rows)
            for n in range(width):
                total = part[n, near, :].astype(F32) + rs1[stage, 0, n, where, :].astype(F32)
                total += rs2[stage, n, where, :].astype(F32)
                for i in range(cuts):
                    acc[i, pl.ds(base + j * rs_rows * width + n, rs_rows, stride=width), :] = (
                        total[:, i * lanes:(i + 1) * lanes])
            high = pl.ds(j * rs_rows * width, rs_rows * width)
            whole = jnp.concatenate(
                [acc[i, pl.ds(base + j * rs_rows * width, rs_rows * width), :] for i in range(cuts)], axis=1)
            nl_own[stage, high, :] = whole.astype(BF16)
            nl_out[stage, where] = whole.reshape(rs_rows, width, chi).astype(BF16)
            send(("up", stage, j), nl_own.at[stage, high, :], nl_in.at[stage, high, :], to_up, when=shifts)
            keep(("up", stage, j), nl_own.at[stage, high, :], nl_in.at[stage, high, :], rests)

    my_half = pl.ds(pl.multiple_of(core * hrows, hrows), hrows)
    mate_half = pl.ds(pl.multiple_of((1 - core) * hrows, hrows), hrows)
    nl_slots = [slot(("nl_land", h)) for h in range(2)]
    assert nl_slots[1] == nl_slots[0] + 1
    nl_land = nl_slots[0] + core
    n_out = 4
    out_slots = [[slot(("out_land", h, j)) for j in range(n_out)] for h in range(2)]
    out_rows = hrows // n_out

    def home_left(stage):
        src, dst = nl_out.at[stage], new_left.at[my_half]
        if stage == 0:
            send(("nl0", 0), src, dst, to_x, when=stays, land=nl_land)
            send(("nl0", 1), src, dst, to_xc, when=moves, land=nl_land)
        else:
            send(("nl1", 0), src, dst, to_c, when=moves, land=nl_land)
            keep(("nl1", 1), src, dst, stays, land=nl_land)

    def home_product(stage, j):
        start = core * hrows + j * out_rows
        dst = product.at[pl.ds(pl.multiple_of(start, out_rows), out_rows)]
        src = prod.at[stage, pl.ds(j * out_rows, out_rows)]
        land = out_slots[0][j] + core * n_out
        if stage == 0:
            send(("out0", j, 0), src, dst, to_xc, when=stays, land=land)
            send(("out0", j, 1), src, dst, to_x, when=moves, land=land)
        else:
            send(("out1", j, 0), src, dst, to_c, when=stays, land=land)
            keep(("out1", j, 1), src, dst, moves, land=land)

    def finalize():
        for key in list(started):
            if key[0] not in ("nl0", "nl1", "out0", "out1") and key not in landed:
                arrive(key, lands[key])
        for h in range(2):
            where = pl.ds(h * hrows, hrows)
            for stage, when in ((0, moves), (1, stays)):
                if (f"nl{stage}", 0) in started:
                    pl.when(when)(functools.partial(arrive, ("nl_land", h), new_left.at[where]))
            for stage, when in ((0, stays), (1, moves)):
                for j in range(n_out):
                    if (f"out{stage}", j, 0) in started:
                        where = pl.ds(h * hrows + j * out_rows, out_rows)
                        pl.when(when)(functools.partial(arrive, ("out_land", h, j), product.at[where]))
        for copies in started.values():
            for copy, when in copies:
                if when is None:
                    copy.wait_send()
                else:
                    pl.when(when)(copy.wait_send)

    partial(0)
    swap_halves(0)
    partial(1)
    add_far(0)
    swap_halves(1)
    send_far(0)
    spread_if(0, moves, True)

    side = width * pq
    col = iota((small, side), 1)
    col_m = lax.rem(col, width)
    col_sv = lax.rem(lax.div(col, width), pq // 2) * 2 + lax.div(col, width * (pq // 2))
    col_s, col_v = lax.div(col_sv, phys), lax.rem(col_sv, phys)
    row = iota((side, small), 0)
    row_k, row_u, row_w = lax.div(row, pq), lax.rem(lax.div(row, phys), phys), lax.rem(row, phys)
    code_c, code_r = iota((small, side), 0), iota((side, small), 1)
    t1 = mm(mpo[...], one_hot(col_s * width + col_m == code_c)).astype(BF16)
    t2 = mm(one_hot(row_w * width + row_k == code_r), mpo[...]).astype(BF16)
    both = jnp.zeros((side, side), F32)
    for n in range(width):
        near = mm(one_hot(row_u * width + n == code_r), t1)
        both += near * mm(t2, one_hot(col_v * width + n == code_c))
    pair[...] = both.astype(BF16)

    add_far(1)
    spread_if(1, moves, True)
    finish(0)
    home_left(0)
    spread_if(2, moves, False)
    relay(0)
    arrive(("right",), right)
    for i in range(cuts):
        acc[i, batch * pq:2 * batch * pq, :] = jnp.zeros((batch * pq, lanes), F32)

    def contract(stage, q):
        ours = nl_in[stage]
        for t in range(pq // 2):
            mixed[t] = mm(ours, psi[q, t])

    def project(p):
        here = mixed[:, p * 2 * width:(p + 1) * 2 * width, :]
        tiles = []
        for i in range(2):
            one = here[:, i * width:(i + 1) * width, :].reshape(pq // 2 * width, 2 * lanes)
            tiles.append(jnp.concatenate([one[:, :lanes], one[:, lanes:]], axis=0))
        both = jnp.concatenate(tiles, axis=1).astype(BF16)
        out = mm(pair[...], both).astype(BF16)
        for i in range(2):
            where = pl.ds((p * 2 + i) * pq, pq)
            for k in range(width):
                proj[where, k * lanes:(k + 1) * lanes] = out[k * pq:(k + 1) * pq, i * lanes:(i + 1) * lanes]

    def environment(q):
        start = q * lanes if isinstance(q, int) else pl.multiple_of(q * lanes, lanes)
        return right[:, pl.ds(start, lanes), :].reshape(width * lanes, chi)

    def gathered(where):
        return jnp.concatenate([acc[i, where, :] for i in range(cuts)], axis=1)

    def strip_of(stage, q):
        contract(stage, q)
        for p in range(batch // 2):
            project(p)
        total = mm(proj[...], environment(q))
        where = pl.ds(stage * batch * pq, batch * pq)
        if not isinstance(q, int) or q > 0:
            total += gathered(where)
        for i in range(cuts):
            acc[i, where, :] = total[:, i * lanes:(i + 1) * lanes]

    def last_strip(stage):
        q = cuts - 1
        contract(stage, q)
        high = out_rows * pq
        for j in range(n_out):
            for p in range(out_rows // 2):
                project(j * (out_rows // 2) + p)
            total = mm(proj[j * high:(j + 1) * high, :], environment(q))
            total += gathered(pl.ds(stage * batch * pq + j * high, high))
            out = total.reshape(out_rows, phys, phys, chi).astype(BF16)
            prod[stage, j * out_rows:(j + 1) * out_rows] = out
            home_product(stage, j)

    complete(0)
    spread_if(2, stays, False)
    spread_if(3, moves, False)
    for j in range(n_rs):
        high = pl.ds(j * rs_rows * width, rs_rows * width)
        arrive(("up", 0, j), nl_in.at[0, high, :])
    strip_of(0, 0)
    relay(1)
    complete(1)
    spread_if(3, stays, False)
    spread_reg(2)
    spread_reg(3)
    strip_of(0, 1)
    relay(2)
    complete(2)
    strip_of(0, 2)
    send_far(1, moves)
    relay(3)
    complete(3)
    send_far(1, stays)
    last_strip(0)
    finish(1)
    home_left(1)
    for j in range(n_rs):
        high = pl.ds(j * rs_rows * width, rs_rows * width)
        arrive(("up", 1, j), nl_in.at[1, high, :])

    @pl.loop(0, cuts - 1)
    def _(q):
        strip_of(1, q)

    last_strip(1)

    finalize()


def fused(left_env, site, psi, right_env, mpo):
    _, rows, width, chi = left_env.shape
    phys = site.shape[2]
    pq = phys * phys
    group, cuts, batch = 16, 4, rows // 2
    lanes = chi // cuts
    small = phys * width
    table = mpo.transpose(3, 1, 2, 0).reshape(small, small)
    n_sems = 120
    any_spec = pl.BlockSpec(memory_space=pl.ANY)
    vmem = pl.BlockSpec(memory_space=pltpu.VMEM)
    new_left, product = pl.pallas_call(
        functools.partial(kernel, (rows, width, phys, chi, group, cuts, batch)),
        out_shape=(
            jax.ShapeDtypeStruct((rows, width, chi), BF16),
            jax.ShapeDtypeStruct((rows, phys, phys, chi), BF16),
        ),
        in_specs=[any_spec] * 5,
        out_specs=(vmem, vmem),
        scratch_shapes=[
            pltpu.VMEM((rows, width, chi), BF16),
            pltpu.VMEM((rows, phys, chi), BF16),
            pltpu.VMEM((rows, phys, phys, chi), BF16),
            pltpu.VMEM((small, small), BF16),
            pltpu.VMEM((width, chi, chi), BF16),
            pltpu.VMEM((phys, rows, chi), BF16),
            pltpu.VMEM((cuts, pq // 2, rows, 2 * lanes), BF16),
            pltpu.VMEM((phys, chi, chi), BF16),
            pltpu.VMEM((chi, phys * rows), BF16),
            pltpu.VMEM((small * group, small * group), BF16),
            pltpu.VMEM((width * pq, width * pq), BF16),
            pltpu.VMEM((width, phys * rows, chi), BF16),
            pltpu.VMEM((width, chi, chi), BF16),
            pltpu.VMEM((2, 2, width, rows // 2, chi), BF16),
            pltpu.VMEM((2, width, rows // 2, chi), BF16),
            pltpu.VMEM((2, width, rows // 2, chi), BF16),
            pltpu.VMEM((2, rows // 2 * width, chi), BF16),
            pltpu.VMEM((2, rows // 2, width, chi), BF16),
            pltpu.VMEM((2, rows // 2 * width, chi), BF16),
            pltpu.VMEM((cuts, pq // 2, chi, 2 * lanes), BF16),
            pltpu.VMEM((pq // 2, batch * width, 2 * lanes), F32),
            pltpu.VMEM((batch * pq, width * lanes), BF16),
            pltpu.VMEM((2, rows // 2, phys, phys, chi), BF16),
            pltpu.VMEM((cuts, rows * pq, lanes), F32),
            pltpu.SemaphoreType.DMA((6,)),
            pltpu.SemaphoreType.DMA((n_sems,)),
            pltpu.SemaphoreType.DMA((n_sems,)),
        ],
        compiler_params=pltpu.CompilerParams(
            collective_id=0, has_side_effects=True, vmem_limit_bytes=62 * 1024 * 1024
        ),
    )(left_env[0], site[0], psi[0], right_env[0], table)
    return new_left[None], product[None]


def shifted(block, axis, distance):
    devices = range(lax.axis_size(axis))
    route = [((i - distance) % len(devices), i) for i in devices]
    return lax.ppermute(block, axis, route)


def shards(left_env, site, psi, right_env, mpo):
    left = left_env[0]
    tensor = site[0]
    rows = tensor.shape[0]
    phys = tensor.shape[1]
    chi = tensor.shape[2]
    width = left.shape[1]
    pair_source = shifted(psi[0], "sec", 1)
    offset = lax.axis_index("bond") * rows
    whole_left, whole_site = (
        lax.all_gather(left, "bond", axis=0, tiled=True),
        lax.all_gather(tensor, "bond", axis=0, tiled=True),
    )
    own_cols = lax.dynamic_slice_in_dim(whole_site, offset, rows, 2)
    first = jnp.dot(
        whole_left.reshape(chi * width, chi),
        own_cols.reshape(chi, phys * rows),
        preferred_element_type=jnp.float32,
    )
    first = first.astype(jnp.bfloat16).reshape(chi, width, phys, rows)
    second = jnp.einsum("pmsb,mnsu->punb", first, mpo, preferred_element_type=jnp.float32).astype(
        jnp.bfloat16
    )
    fresh = lax.dot_general(
        whole_site.reshape(chi * phys, chi),
        second.reshape(chi * phys, width * rows),
        (((0,), (0,)), ((), ())),
        preferred_element_type=jnp.float32,
    )
    fresh = fresh.astype(jnp.bfloat16).reshape(chi, width, rows)
    new_left = lax.all_to_all(fresh, "bond", split_axis=0, concat_axis=2, tiled=True)
    left_source = shifted(new_left, "sec", 1)
    source_flat = left_source.reshape(rows * width, chi)
    pair = pair_source.reshape(rows, phys * phys * chi)
    mixed = jnp.dot(
        source_flat,
        lax.all_gather(pair, "bond", axis=0, tiled=True),
        preferred_element_type=jnp.float32,
    )
    mixed = mixed.astype(jnp.bfloat16).reshape(rows, width * phys * phys, chi)
    two_site = jnp.einsum("mnsu,nkvw->msvuwk", mpo, mpo, preferred_element_type=jnp.float32)
    two_site = two_site.astype(jnp.bfloat16).reshape(width * phys * phys, phys * phys * width)
    projected = jnp.einsum(
        "pqc,qr->prc", mixed, two_site, preferred_element_type=jnp.float32
    ).astype(jnp.bfloat16)
    env_right = right_env[0].reshape(width * chi, chi)
    result = jnp.dot(
        projected.reshape(rows * phys * phys, width * chi),
        env_right,
        preferred_element_type=jnp.float32,
    ).astype(jnp.bfloat16)
    return (new_left[None], result.reshape(1, rows, phys, phys, chi))


def solution(mesh):
    in_specs = (
        P("sec", "bond", None, None),
        P("sec", "bond", None, None),
        P("sec", "bond", None, None, None),
        P("sec", None, None, None),
        P(),
    )
    out_specs = (P("sec", "bond", None, None), P("sec", "bond", None, None, None))
    body = fused if mesh.shape["bond"] == 4 else shards
    return jax.shard_map(body, mesh=mesh, in_specs=in_specs, out_specs=out_specs, check_vma=False)
```

```python
import functools

import jax
import jax.numpy as jnp
from jax import lax
from jax.experimental import pallas as pl
from jax.experimental.pallas import tpu as pltpu
from jax.sharding import PartitionSpec as P

MESH = pl.DeviceIdType.MESH
BF16 = jnp.bfloat16
F32 = jnp.float32


def mm(a, b):
    return jnp.dot(a, b, preferred_element_type=F32)


def kernel(
    dims,
    left_h, site_h, psi_h, right_h, mpo_h,
    new_left, product,
    left, site_raw, psi_raw, mpo_raw, mpo_f, mpo, right,
    site_own, psi_own, site, site_tr, mix, pair,
    second, part, rs1, send2, rs2, nl_own, nl_out, nl_in, psi, mixed, proj, prod, acc,
    local_sem, send_sem, recv_sem,
):
    rows, width, phys, chi, group, cuts, batch = dims
    pq = phys * phys
    n_sec = lax.axis_size("sec")
    sec = lax.axis_index("sec")
    me = lax.axis_index("bond")
    x, y = lax.rem(me, 2), me // 2
    core, z = lax.rem(sec, 2), sec // 2
    mate_sec = 2 * z + 1 - core
    side_bond = 2 * y + 1 - x
    to_c = {"sec": mate_sec}
    to_y = {"bond": 2 * (1 - y) + x}
    to_x = {"bond": side_bond}
    to_xc = {"sec": mate_sec, "bond": side_bond}
    up = lax.rem(sec + 2, n_sec)
    to_up = {"sec": up}
    stays = x == core
    moves = x != core
    shifts = x == 1
    rests = x == 0

    mine = 2 * y + core
    mates = 2 * y + 1 - core
    across = 2 * (1 - y) + core
    corner = 2 * (1 - y) + 1 - core

    def block(owner):
        return pl.ds(pl.multiple_of(owner * rows, rows), rows)

    loads = {}
    for i, (name, src, dst) in enumerate((
        ("site", site_h, site_raw),
        ("psi", psi_h, psi_raw),
        ("mpo", mpo_h, mpo_raw),
    )):
        loads[name] = pltpu.make_async_copy(src, dst, local_sem.at[i])
        loads[name].start()

    barrier = pltpu.get_barrier_semaphore()
    greeted = [to_c, to_y, to_x, to_xc]
    for dz in (2, n_sec - 2):
        greeted.append({"sec": lax.rem(sec + dz, n_sec)})
        greeted.append({"sec": lax.rem(mate_sec + dz, n_sec), "bond": side_bond})
    for target in greeted:
        pl.semaphore_signal(barrier, inc=1, device_id=target, device_id_type=MESH)

    lanes = chi // cuts
    loads["site"].wait()
    flat = site_raw[...].astype(F32).reshape(rows * phys, chi)
    for i in range(cuts):
        acc[i, :rows * phys, :] = flat[:, i * lanes:(i + 1) * lanes]
    for t in range(phys):
        for i in range(cuts):
            tile = acc[i, pl.ds(t, rows, stride=phys), :]
            site_own[t, :, i * lanes:(i + 1) * lanes] = tile.astype(BF16)

    started = {}
    counter = {}
    lands = {}
    landed = set()

    def slot(key):
        return counter.setdefault(key, len(counter))

    def remote(i, j, src, dst, target):
        return pltpu.make_async_remote_copy(
            src_ref=src, dst_ref=dst, send_sem=send_sem.at[i], recv_sem=recv_sem.at[j],
            device_id=target, device_id_type=MESH,
        )

    def send(key, src, dst, target, when=None, land=None):
        i = slot(key)
        copy = remote(i, i if land is None else land, src, dst, target)
        if when is None:
            copy.start()
        else:
            pl.when(when)(copy.start)
        started.setdefault(key, []).append((copy, when))
        lands[key] = dst

    def keep(key, src, dst, when, land=None):
        copy = pltpu.make_async_copy(src, dst, recv_sem.at[slot(key) if land is None else land])
        pl.when(when)(copy.start)

    def arrive(key, dst):
        i = slot(key)
        landed.add(key)
        remote(i, i, dst, dst, to_c).wait_recv()

    pieces = tuple(pl.ds(t, 1) for t in range(phys))
    n_left = 4
    tall_left = rows // n_left

    def left_part(i):
        return pl.ds(i * tall_left, tall_left)

    def send_left(i):
        send(("left", i), left_h.at[left_part(i)], left.at[left_part(i)], to_xc, when=moves)
        keep(("left", i), left_h.at[left_part(i)], left.at[left_part(i)], stays)

    pl.semaphore_wait(barrier, len(greeted))

    def site_spread(p, from_own):
        src = site_own.at[pieces[p]] if from_own else site.at[pieces[p], block(mine), :]
        when = stays if from_own else None
        send(("site_y", p), src, site.at[pieces[p], block(mine), :], to_y, when)
        send(("site_c", p), src, site.at[pieces[p], block(mine), :], to_c, when)

    for p in range(phys):
        send(("site", p), site_own.at[pieces[p]], site.at[pieces[p], block(me), :], to_xc, when=moves)
        keep(("site", p), site_own.at[pieces[p]], site.at[pieces[p], block(me), :], stays)
        site_spread(p, True)
    for i in range(n_left):
        send_left(i)

    loads["psi"].wait()
    tall = 8

    @pl.loop(0, rows // tall)
    def _(g):
        flat = psi_raw[pl.ds(pl.multiple_of(g * tall, tall), tall)].astype(F32)
        flat = flat.reshape(tall * pq, chi)
        where = pl.ds(pl.multiple_of(g * tall * pq, tall * pq), tall * pq)
        for i in range(cuts):
            acc[i, where, :] = flat[:, i * lanes:(i + 1) * lanes]

    def region(q, owner):
        return psi.at[q, :, block(owner), :]

    psi_self = jnp.logical_and(x == 0, core == 0)
    to_psi = {
        "sec": lax.rem(2 * z + x + 2 * core, n_sec),
        "bond": 2 * y + core,
    }

    psi_waits = jnp.logical_and(x == 0, core == 1)
    psi_now = x == 1

    def launch(q):
        send(("own", q), psi_own.at[q], region(q, me), to_psi, when=psi_now)
        keep(("own", q), psi_own.at[q], region(q, me), psi_self)

    def launch_late(q):
        send(("own", q), psi_own.at[q], region(q, me), to_psi, when=psi_waits)

    for q in range(cuts):
        for t in range(pq):
            at = (t % 2) * lanes
            tile = acc[q, pl.ds(t, rows, stride=pq), :]
            psi_own[q, t // 2, :, at:at + lanes] = tile.astype(BF16)
        if q > 0:
            launch(q - 1)
    launch(cuts - 1)

    def spread_if(q, when, last):
        @pl.when(when)
        def _():
            arrive(("own", q), region(q, mine))
            for key, target in (("psi_y", to_y), ("psi_c", to_c)):
                i = slot((key, q))
                remote(i, i, region(q, mine), region(q, mine), target).start()
        if last:
            spread_reg(q)

    stays_up = jnp.logical_and(x == 1, core == 1)

    def spread_reg(q):
        if True:
            for key, target in (("psi_y", to_y), ("psi_c", to_c)):
                i = slot((key, q))
                started[(key, q)] = [(remote(i, i, region(q, mine), region(q, mine), target), None)]
                lands[(key, q)] = region(q, mine)

    def relay(q):
        arrive(("psi_y", q), region(q, across))
        send(("psi_yc", q), region(q, across), region(q, across), to_c)

    def complete(q):
        arrive(("psi_c", q), region(q, mates))
        arrive(("psi_yc", q), region(q, corner))


    @pl.when(moves)
    def _():
        for p in range(phys):
            arrive(("site", p), site.at[pieces[p], block(mine), :])
            src = site.at[pieces[p], block(mine), :]
            remote(slot(("site_y", p)), slot(("site_y", p)), src, src, to_y).start()
            remote(slot(("site_c", p)), slot(("site_c", p)), src, src, to_c).start()

    @pl.when(stays)
    def _():
        for p in range(phys):
            arrive(("site", p), site.at[pieces[p], block(mine), :])

    for p in range(phys):
        for key, target in (("site_y", to_y), ("site_c", to_c)):
            src = site.at[pieces[p], block(mine), :]
            i = slot((key, p))
            started[(key, p)] = [(remote(i, i, src, src, target), None)]

    loads["mpo"].wait()

    def iota(shape, axis):
        return lax.broadcasted_iota(jnp.int32, shape, axis)

    def one_hot(condition):
        return jnp.where(condition, 1.0, 0.0).astype(BF16)

    small = phys * width
    codes = width * width
    pick_n = one_hot(lax.rem(iota((width, codes), 1), width) == iota((width, codes), 0))
    same_m = lax.div(iota((codes, small), 0), width) == lax.rem(iota((codes, small), 1), width)
    for u in range(phys):
        col_s = lax.div(iota((pq, small), 1), width)
        spread_s = one_hot(iota((pq, small), 0) == col_s * phys + u)
        chosen = jnp.where(same_m, mm(mpo_raw[...], spread_s), 0.0).astype(BF16)
        mpo_f[u * width:(u + 1) * width, :] = mm(pick_n, chosen)
    mpo[...] = mpo_f[...].astype(BF16)
    big = small * group
    tall_code = lax.div(iota((big, small), 0), group)
    spread_rows = one_hot(tall_code == iota((big, small), 1))
    col = iota((small, big), 1)
    col_code = lax.div(col, group * width) * width + lax.rem(col, width)
    spread_cols = one_hot(col_code == iota((small, big), 0))
    wide = mm(mm(spread_rows, mpo[...]).astype(BF16), spread_cols)
    same = lax.rem(iota((big, big), 0), group) == lax.rem(lax.div(iota((big, big), 1), width), group)
    mix[...] = jnp.where(same, wide, 0.0).astype(BF16)

    for t in range(phys):
        own = site[t, block(mine), :].astype(F32)
        for i in range(cuts):
            tile = own[:, i * lanes:(i + 1) * lanes]
            site_tr[i * lanes:(i + 1) * lanes, t * rows:(t + 1) * rows] = tile.T.astype(BF16)

    spread_if(0, stays, False)
    for p in range(phys):
        arrive(("site_y", p), site.at[pieces[p], block(across), :])
        send(("site_yc", p), site.at[pieces[p], block(across), :], site.at[pieces[p], block(across), :], to_c)

    spread_if(1, psi_self, False)
    for p in range(phys):
        arrive(("site_c", p), site.at[pieces[p], block(mates), :])
        arrive(("site_yc", p), site.at[pieces[p], block(corner), :])

    send(("right",), right_h, right, to_c, when=moves)
    keep(("right",), right_h, right, moves)
    strip = group * width
    per_left = tall_left // group

    for i in range(n_left):
        arrive(("left", i), left.at[left_part(i)])

        @pl.loop(i * per_left, (i + 1) * per_left, unroll=per_left)
        def _(g):
            ours = left[pl.ds(pl.multiple_of(g * group, group), group)].astype(F32)
            ours = ours.reshape(strip, chi).astype(BF16)
            first = jnp.concatenate([mm(ours, site[s]).astype(BF16) for s in range(phys)], axis=0)
            out = mm(mix[...], first).astype(BF16)
            for u in range(phys):
                for n in range(width):
                    at = (u * width + n) * group
                    where = pl.multiple_of(u * rows + g * group, group)
                    second[n, pl.ds(where, group), :] = out[at:at + group, :]

        if i == 0:
            spread_if(1, stays_up, False)
        if i == n_left - 2:
            for q in range(cuts):
                launch_late(q)
            spread_if(2, stays, False)


    hrows = rows // 2

    def rows_of(stage, far, half):
        yy = 1 - y if far else y
        column = 1 - x if stage == 0 else x
        start = (2 * yy + column) * rows + half * hrows
        return pl.ds(pl.multiple_of(start, hrows), hrows)

    def block_of(stage, far):
        yy = 1 - y if far else y
        column = 1 - x if stage == 0 else x
        return block(2 * yy + column)

    def partial(stage):
        for far in (1, 0):
            where = block_of(stage, far)
            for n in range(width):
                part[n, where, :] = mm(site_tr[where, :], second[n]).astype(BF16)

    def swap_halves(stage):
        for far in (1, 0):
            send(("rs1", stage, far), part.at[:, rows_of(stage, far, 1 - core), :], rs1.at[stage, far], to_c)

    n_rs = 4
    rs_rows = hrows // n_rs

    def add_far(stage):
        arrive(("rs1", stage, 1), rs1.at[stage, 1])
        for n in range(width):
            total = part[n, rows_of(stage, 1, core), :].astype(F32) + rs1[stage, 1, n].astype(F32)
            send2[stage, n] = total.astype(BF16)

    def send_far(stage, when=None):
        for j in range(n_rs):
            where = pl.ds(j * rs_rows, rs_rows)
            send(("rs2", stage, j), send2.at[stage, :, where, :], rs2.at[stage, :, where, :], to_y, when=when)

    def finish(stage, parts):
        if parts[0] == 0:
            arrive(("rs1", stage, 0), rs1.at[stage, 0])
        base = stage * hrows * width
        for j in parts:
            where = pl.ds(j * rs_rows, rs_rows)
            arrive(("rs2", stage, j), rs2.at[stage, :, where, :])
            yy = y
            column = 1 - x if stage == 0 else x
            start = (2 * yy + column) * rows + core * hrows + j * rs_rows
            near = pl.ds(pl.multiple_of(start, rs_rows), rs_rows)
            for n in range(width):
                total = part[n, near, :].astype(F32) + rs1[stage, 0, n, where, :].astype(F32)
                total += rs2[stage, n, where, :].astype(F32)
                for i in range(cuts):
                    acc[i, pl.ds(base + j * rs_rows * width + n, rs_rows, stride=width), :] = (
                        total[:, i * lanes:(i + 1) * lanes])
            high = pl.ds(j * rs_rows * width, rs_rows * width)
            whole = jnp.concatenate(
                [acc[i, pl.ds(base + j * rs_rows * width, rs_rows * width), :] for i in range(cuts)], axis=1)
            nl_own[stage, high, :] = whole.astype(BF16)
            nl_out[stage, where] = whole.reshape(rs_rows, width, chi).astype(BF16)
            send(("up", stage, j), nl_own.at[stage, high, :], nl_in.at[stage, high, :], to_up, when=shifts)
            keep(("up", stage, j), nl_own.at[stage, high, :], nl_in.at[stage, high, :], rests)

    my_half = pl.ds(pl.multiple_of(core * hrows, hrows), hrows)
    mate_half = pl.ds(pl.multiple_of((1 - core) * hrows, hrows), hrows)
    nl_slots = [slot(("nl_land", h)) for h in range(2)]
    assert nl_slots[1] == nl_slots[0] + 1
    nl_land = nl_slots[0] + core
    n_out = 4
    out_slots = [[slot(("out_land", h, j)) for j in range(n_out)] for h in range(2)]
    out_rows = hrows // n_out

    def home_left(stage):
        src, dst = nl_out.at[stage], new_left.at[my_half]
        if stage == 0:
            send(("nl0", 0), src, dst, to_x, when=stays, land=nl_land)
            send(("nl0", 1), src, dst, to_xc, when=moves, land=nl_land)
        else:
            send(("nl1", 0), src, dst, to_c, when=moves, land=nl_land)
            keep(("nl1", 1), src, dst, stays, land=nl_land)

    def home_product(stage, j):
        start = core * hrows + j * out_rows
        dst = product.at[pl.ds(pl.multiple_of(start, out_rows), out_rows)]
        src = prod.at[stage, pl.ds(j * out_rows, out_rows)]
        land = out_slots[0][j] + core * n_out
        if stage == 0:
            send(("out0", j, 0), src, dst, to_xc, when=stays, land=land)
            send(("out0", j, 1), src, dst, to_x, when=moves, land=land)
        else:
            send(("out1", j, 0), src, dst, to_c, when=stays, land=land)
            keep(("out1", j, 1), src, dst, moves, land=land)

    def finalize():
        for key in list(started):
            if key[0] not in ("nl0", "nl1", "out0", "out1") and key not in landed:
                arrive(key, lands[key])
        for h in range(2):
            where = pl.ds(h * hrows, hrows)
            for stage, when in ((0, moves), (1, stays)):
                if (f"nl{stage}", 0) in started:
                    pl.when(when)(functools.partial(arrive, ("nl_land", h), new_left.at[where]))
            for stage, when in ((0, stays), (1, moves)):
                for j in range(n_out):
                    if (f"out{stage}", j, 0) in started:
                        where = pl.ds(h * hrows + j * out_rows, out_rows)
                        pl.when(when)(functools.partial(arrive, ("out_land", h, j), product.at[where]))
        for copies in started.values():
            for copy, when in copies:
                if when is None:
                    copy.wait_send()
                else:
                    pl.when(when)(copy.wait_send)

    partial(0)
    swap_halves(0)
    partial(1)
    add_far(0)
    swap_halves(1)
    send_far(0)
    spread_if(0, moves, True)

    side = width * pq
    col = iota((small, side), 1)
    col_m = lax.rem(col, width)
    col_sv = lax.rem(lax.div(col, width), pq // 2) * 2 + lax.div(col, width * (pq // 2))
    col_s, col_v = lax.div(col_sv, phys), lax.rem(col_sv, phys)
    row = iota((side, small), 0)
    row_k, row_u, row_w = lax.div(row, pq), lax.rem(lax.div(row, phys), phys), lax.rem(row, phys)
    code_c, code_r = iota((small, side), 0), iota((side, small), 1)
    t1 = mm(mpo[...], one_hot(col_s * width + col_m == code_c)).astype(BF16)
    t2 = mm(one_hot(row_w * width + row_k == code_r), mpo[...]).astype(BF16)
    both = jnp.zeros((side, side), F32)
    for n in range(width):
        near = mm(one_hot(row_u * width + n == code_r), t1)
        both += near * mm(t2, one_hot(col_v * width + n == code_c))
    pair[...] = both.astype(BF16)

    add_far(1)
    spread_if(1, moves, True)
    finish(0, range(n_rs))
    home_left(0)
    spread_if(2, moves, False)
    relay(0)
    arrive(("right",), right)
    for i in range(cuts):
        acc[i, batch * pq:2 * batch * pq, :] = jnp.zeros((batch * pq, lanes), F32)

    def contract(stage, q, lo, n):
        ours = nl_in[stage, lo * width:(lo + n) * width, :]
        for t in range(pq // 2):
            mixed[t, :n * width, :] = mm(ours, psi[q, t])

    def project(p):
        here = mixed[:, p * 2 * width:(p + 1) * 2 * width, :]
        tiles = []
        for i in range(2):
            one = here[:, i * width:(i + 1) * width, :].reshape(pq // 2 * width, 2 * lanes)
            tiles.append(jnp.concatenate([one[:, :lanes], one[:, lanes:]], axis=0))
        both = jnp.concatenate(tiles, axis=1).astype(BF16)
        out = mm(pair[...], both).astype(BF16)
        for i in range(2):
            where = pl.ds((p * 2 + i) * pq, pq)
            for k in range(width):
                proj[where, k * lanes:(k + 1) * lanes] = out[k * pq:(k + 1) * pq, i * lanes:(i + 1) * lanes]

    def environment(q):
        start = q * lanes if isinstance(q, int) else pl.multiple_of(q * lanes, lanes)
        return right[:, pl.ds(start, lanes), :].reshape(width * lanes, chi)

    def gathered(where):
        return jnp.concatenate([acc[i, where, :] for i in range(cuts)], axis=1)

    def strip_of(stage, q, lo=0, n=None):
        n = batch if n is None else n
        contract(stage, q, lo, n)
        for p in range(n // 2):
            project(p)
        total = mm(proj[:n * pq, :], environment(q))
        where = pl.ds((stage * batch + lo) * pq, n * pq)
        if not isinstance(q, int) or q > 0:
            total += gathered(where)
        for i in range(cuts):
            acc[i, where, :] = total[:, i * lanes:(i + 1) * lanes]

    def last_strip(stage, lo=0, n=None):
        n = batch if n is None else n
        q = cuts - 1
        contract(stage, q, lo, n)
        high = out_rows * pq
        for j in range(n // out_rows):
            for p in range(out_rows // 2):
                project(j * (out_rows // 2) + p)
            total = mm(proj[j * high:(j + 1) * high, :], environment(q))
            total += gathered(pl.ds((stage * batch + lo) * pq + j * high, high))
            out = total.reshape(out_rows, phys, phys, chi).astype(BF16)
            prod[stage, lo + j * out_rows:lo + (j + 1) * out_rows] = out
            home_product(stage, lo // out_rows + j)

    complete(0)
    spread_if(3, moves, False)
    for j in range(n_rs):
        high = pl.ds(j * rs_rows * width, rs_rows * width)
        arrive(("up", 0, j), nl_in.at[0, high, :])
    strip_of(0, 0)
    relay(1)
    complete(1)
    spread_if(3, stays, False)
    spread_reg(2)
    spread_reg(3)
    strip_of(0, 1)
    relay(2)
    complete(2)
    strip_of(0, 2)
    send_far(1, moves)
    relay(3)
    complete(3)
    send_far(1, stays)
    last_strip(0)
    def landed_rows(stage, parts):
        for j in parts:
            high = pl.ds(j * rs_rows * width, rs_rows * width)
            arrive(("up", stage, j), nl_in.at[stage, high, :])

    few = batch // 2
    early_parts, late_parts = range(n_rs // 2), range(n_rs // 2, n_rs)
    finish(1, early_parts)
    landed_rows(1, early_parts)

    @pl.loop(0, cuts // 2)
    def _(q):
        strip_of(1, q, 0, few)

    finish(1, late_parts)
    home_left(1)
    for q in range(cuts // 2, cuts - 1):
        strip_of(1, q, 0, few)
    last_strip(1, 0, few)
    landed_rows(1, late_parts)

    @pl.loop(0, cuts - 1)
    def _(q):
        strip_of(1, q, few, few)

    last_strip(1, few, few)
    finalize()


def fused(left_env, site, psi, right_env, mpo):
    _, rows, width, chi = left_env.shape
    phys = site.shape[2]
    pq = phys * phys
    group, cuts, batch = 16, 4, rows // 2
    lanes = chi // cuts
    small = phys * width
    table = mpo.reshape(width * width, pq)
    n_sems = 120
    any_spec = pl.BlockSpec(memory_space=pl.ANY)
    new_left, product = pl.pallas_call(
        functools.partial(kernel, (rows, width, phys, chi, group, cuts, batch)),
        out_shape=(
            jax.ShapeDtypeStruct((rows, width, chi), BF16),
            jax.ShapeDtypeStruct((rows, phys, phys, chi), BF16),
        ),
        in_specs=[any_spec] * 5,
        out_specs=(any_spec, any_spec),
        scratch_shapes=[
            pltpu.VMEM((rows, width, chi), BF16),
            pltpu.VMEM((rows, phys, chi), BF16),
            pltpu.VMEM((rows, phys, phys, chi), BF16),
            pltpu.VMEM((width * width, pq), BF16),
            pltpu.VMEM((small, small), F32),
            pltpu.VMEM((small, small), BF16),
            pltpu.VMEM((width, chi, chi), BF16),
            pltpu.VMEM((phys, rows, chi), BF16),
            pltpu.VMEM((cuts, pq // 2, rows, 2 * lanes), BF16),
            pltpu.VMEM((phys, chi, chi), BF16),
            pltpu.VMEM((chi, phys * rows), BF16),
            pltpu.VMEM((small * group, small * group), BF16),
            pltpu.VMEM((width * pq, width * pq), BF16),
            pltpu.VMEM((width, phys * rows, chi), BF16),
            pltpu.VMEM((width, chi, chi), BF16),
            pltpu.VMEM((2, 2, width, rows // 2, chi), BF16),
            pltpu.VMEM((2, width, rows // 2, chi), BF16),
            pltpu.VMEM((2, width, rows // 2, chi), BF16),
            pltpu.VMEM((2, rows // 2 * width, chi), BF16),
            pltpu.VMEM((2, rows // 2, width, chi), BF16),
            pltpu.VMEM((2, rows // 2 * width, chi), BF16),
            pltpu.VMEM((cuts, pq // 2, chi, 2 * lanes), BF16),
            pltpu.VMEM((pq // 2, batch * width, 2 * lanes), F32),
            pltpu.VMEM((batch * pq, width * lanes), BF16),
            pltpu.VMEM((2, rows // 2, phys, phys, chi), BF16),
            pltpu.VMEM((cuts, rows * pq, lanes), F32),
            pltpu.SemaphoreType.DMA((6,)),
            pltpu.SemaphoreType.DMA((n_sems,)),
            pltpu.SemaphoreType.DMA((n_sems,)),
        ],
        compiler_params=pltpu.CompilerParams(
            collective_id=0, has_side_effects=True, vmem_limit_bytes=62 * 1024 * 1024
        ),
    )(left_env[0], site[0], psi[0], right_env[0], table)
    return new_left[None], product[None]


def shifted(block, axis, distance):
    devices = range(lax.axis_size(axis))
    route = [((i - distance) % len(devices), i) for i in devices]
    return lax.ppermute(block, axis, route)


def shards(left_env, site, psi, right_env, mpo):
    left = left_env[0]
    tensor = site[0]
    rows = tensor.shape[0]
    phys = tensor.shape[1]
    chi = tensor.shape[2]
    width = left.shape[1]
    pair_source = shifted(psi[0], "sec", 1)
    offset = lax.axis_index("bond") * rows
    whole_left, whole_site = (
        lax.all_gather(left, "bond", axis=0, tiled=True),
        lax.all_gather(tensor, "bond", axis=0, tiled=True),
    )
    own_cols = lax.dynamic_slice_in_dim(whole_site, offset, rows, 2)
    first = jnp.dot(
        whole_left.reshape(chi * width, chi),
        own_cols.reshape(chi, phys * rows),
        preferred_element_type=jnp.float32,
    )
    first = first.astype(jnp.bfloat16).reshape(chi, width, phys, rows)
    second = jnp.einsum("pmsb,mnsu->punb", first, mpo, preferred_element_type=jnp.float32).astype(
        jnp.bfloat16
    )
    fresh = lax.dot_general(
        whole_site.reshape(chi * phys, chi),
        second.reshape(chi * phys, width * rows),
        (((0,), (0,)), ((), ())),
        preferred_element_type=jnp.float32,
    )
    fresh = fresh.astype(jnp.bfloat16).reshape(chi, width, rows)
    new_left = lax.all_to_all(fresh, "bond", split_axis=0, concat_axis=2, tiled=True)
    left_source = shifted(new_left, "sec", 1)
    source_flat = left_source.reshape(rows * width, chi)
    pair = pair_source.reshape(rows, phys * phys * chi)
    mixed = jnp.dot(
        source_flat,
        lax.all_gather(pair, "bond", axis=0, tiled=True),
        preferred_element_type=jnp.float32,
    )
    mixed = mixed.astype(jnp.bfloat16).reshape(rows, width * phys * phys, chi)
    two_site = jnp.einsum("mnsu,nkvw->msvuwk", mpo, mpo, preferred_element_type=jnp.float32)
    two_site = two_site.astype(jnp.bfloat16).reshape(width * phys * phys, phys * phys * width)
    projected = jnp.einsum(
        "pqc,qr->prc", mixed, two_site, preferred_element_type=jnp.float32
    ).astype(jnp.bfloat16)
    env_right = right_env[0].reshape(width * chi, chi)
    result = jnp.dot(
        projected.reshape(rows * phys * phys, width * chi),
        env_right,
        preferred_element_type=jnp.float32,
    ).astype(jnp.bfloat16)
    return (new_left[None], result.reshape(1, rows, phys, phys, chi))


def solution(mesh):
    in_specs = (
        P("sec", "bond", None, None),
        P("sec", "bond", None, None),
        P("sec", "bond", None, None, None),
        P("sec", None, None, None),
        P(),
    )
    out_specs = (P("sec", "bond", None, None), P("sec", "bond", None, None, None))
    body = fused if mesh.shape["bond"] == 4 else shards
    return jax.shard_map(body, mesh=mesh, in_specs=in_specs, out_specs=out_specs, check_vma=False)
```

```python
import functools

import jax
import jax.numpy as jnp
from jax import lax
from jax.experimental import pallas as pl
from jax.experimental.pallas import tpu as pltpu
from jax.sharding import PartitionSpec as P

MESH = pl.DeviceIdType.MESH
BF16 = jnp.bfloat16
F32 = jnp.float32


def mm(a, b):
    return jnp.dot(a, b, preferred_element_type=F32)


def kernel(
    dims,
    left_h, site_h, psi_h, right_h, mpo_h,
    new_left, product,
    left, site_raw, psi_raw, mpo_raw, mpo, right,
    site_own, psi_own, site, site_tr, mix, pair,
    second, part, rs1, send2, rs2, nl_own, nl_out, nl_in, psi, mixed, proj, prod, acc,
    local_sem, send_sem, recv_sem, chain,
):
    rows, width, phys, chi, group, cuts, batch = dims
    pq = phys * phys
    n_sec = lax.axis_size("sec")
    sec = lax.axis_index("sec")
    me = lax.axis_index("bond")
    x, y = lax.rem(me, 2), me // 2
    core, z = lax.rem(sec, 2), sec // 2
    mate_sec = 2 * z + 1 - core
    side_bond = 2 * y + 1 - x
    to_c = {"sec": mate_sec}
    to_y = {"bond": 2 * (1 - y) + x}
    to_x = {"bond": side_bond}
    to_xc = {"sec": mate_sec, "bond": side_bond}
    up = lax.rem(sec + 2, n_sec)
    to_up = {"sec": up}
    stays = x == core
    moves = x != core
    shifts = x == 1
    rests = x == 0

    mine = 2 * y + core
    mates = 2 * y + 1 - core
    across = 2 * (1 - y) + core
    corner = 2 * (1 - y) + 1 - core

    def block(owner):
        return pl.ds(pl.multiple_of(owner * rows, rows), rows)

    loads = {}
    for i, (name, src, dst) in enumerate((
        ("site", site_h, site_raw),
        ("psi", psi_h, psi_raw),
        ("mpo", mpo_h, mpo_raw),
    )):
        loads[name] = pltpu.make_async_copy(src, dst, local_sem.at[i])
        loads[name].start()

    barrier = pltpu.get_barrier_semaphore()
    greeted = [to_c, to_y, to_x, to_xc]
    for target in greeted:
        pl.semaphore_signal(barrier, inc=1, device_id=target, device_id_type=MESH)
    top = n_sec // 2 - 1
    down = lax.rem(sec + n_sec - 2, n_sec)
    down_xc = {"sec": lax.rem(mate_sec + n_sec - 2, n_sec), "bond": side_bond}

    def tell(semaphore, target):
        pl.semaphore_signal(semaphore, inc=1, device_id=target, device_id_type=MESH)

    pl.when(jnp.logical_and(x == 1, z > 0))(lambda: tell(barrier, {"sec": down}))
    pl.when(jnp.logical_and(jnp.logical_and(x == 1, core == 0), z > 0))(lambda: tell(barrier, down_xc))
    climbs = jnp.logical_or(x == 1, core == 1)
    below_top = jnp.logical_and(climbs, z < top)

    lanes = chi // cuts
    loads["site"].wait()
    flat = site_raw[...].astype(F32).reshape(rows * phys, chi)
    for i in range(cuts):
        acc[i, :rows * phys, :] = flat[:, i * lanes:(i + 1) * lanes]
    for t in range(phys):
        for i in range(cuts):
            tile = acc[i, pl.ds(t, rows, stride=phys), :]
            site_own[t, :, i * lanes:(i + 1) * lanes] = tile.astype(BF16)

    started = {}
    counter = {}
    lands = {}
    landed = set()

    def slot(key):
        return counter.setdefault(key, len(counter))

    def remote(i, j, src, dst, target):
        return pltpu.make_async_remote_copy(
            src_ref=src, dst_ref=dst, send_sem=send_sem.at[i], recv_sem=recv_sem.at[j],
            device_id=target, device_id_type=MESH,
        )

    def send(key, src, dst, target, when=None, land=None):
        i = slot(key)
        copy = remote(i, i if land is None else land, src, dst, target)
        if when is None:
            copy.start()
        else:
            pl.when(when)(copy.start)
        started.setdefault(key, []).append((copy, when))
        lands[key] = dst

    def keep(key, src, dst, when, land=None):
        copy = pltpu.make_async_copy(src, dst, recv_sem.at[slot(key) if land is None else land])
        pl.when(when)(copy.start)

    def arrive(key, dst):
        i = slot(key)
        landed.add(key)
        remote(i, i, dst, dst, to_c).wait_recv()

    pieces = tuple(pl.ds(t, 1) for t in range(phys))
    n_left = 4
    tall_left = rows // n_left

    def left_part(i):
        return pl.ds(i * tall_left, tall_left)

    def send_left(i):
        send(("left", i), left_h.at[left_part(i)], left.at[left_part(i)], to_xc, when=moves)
        keep(("left", i), left_h.at[left_part(i)], left.at[left_part(i)], stays)

    pl.semaphore_wait(barrier, len(greeted) + jnp.where(below_top, 1, 0))
    pl.when(jnp.logical_and(x == 1, z == 0))(lambda: tell(chain.at[0], {"sec": up}))

    def site_spread(p, from_own):
        src = site_own.at[pieces[p]] if from_own else site.at[pieces[p], block(mine), :]
        when = stays if from_own else None
        send(("site_y", p), src, site.at[pieces[p], block(mine), :], to_y, when)
        send(("site_c", p), src, site.at[pieces[p], block(mine), :], to_c, when)

    for p in range(phys):
        send(("site", p), site_own.at[pieces[p]], site.at[pieces[p], block(me), :], to_xc, when=moves)
        keep(("site", p), site_own.at[pieces[p]], site.at[pieces[p], block(me), :], stays)
        site_spread(p, True)
    for i in range(n_left):
        send_left(i)


    @pl.when(jnp.logical_and(x == 1, jnp.logical_and(z > 0, z < top)))
    def _():
        pl.semaphore_wait(chain.at[0], 1)
        tell(chain.at[0], {"sec": up})

    loads["psi"].wait()
    tall = 8

    @pl.loop(0, rows // tall)
    def _(g):
        flat = psi_raw[pl.ds(pl.multiple_of(g * tall, tall), tall)].astype(F32)
        flat = flat.reshape(tall * pq, chi)
        where = pl.ds(pl.multiple_of(g * tall * pq, tall * pq), tall * pq)
        for i in range(cuts):
            acc[i, where, :] = flat[:, i * lanes:(i + 1) * lanes]

    def region(q, owner):
        return psi.at[q, :, block(owner), :]

    psi_self = jnp.logical_and(x == 0, core == 0)
    to_psi = {
        "sec": lax.rem(2 * z + x + 2 * core, n_sec),
        "bond": 2 * y + core,
    }

    psi_waits = jnp.logical_and(x == 0, core == 1)
    psi_now = x == 1

    def launch(q):
        send(("own", q), psi_own.at[q], region(q, me), to_psi, when=psi_now)
        keep(("own", q), psi_own.at[q], region(q, me), psi_self)

    def launch_late(q):
        send(("own", q), psi_own.at[q], region(q, me), to_psi, when=psi_waits)

    for q in range(cuts):
        for t in range(pq):
            at = (t % 2) * lanes
            tile = acc[q, pl.ds(t, rows, stride=pq), :]
            psi_own[q, t // 2, :, at:at + lanes] = tile.astype(BF16)

    @pl.when(jnp.logical_and(x == 1, z == top))
    def _():
        pl.semaphore_wait(chain.at[0], 1)
        pl.when(core == 0)(lambda: tell(chain.at[1], to_xc))

    for q in range(cuts):
        launch(q)

    def spread_if(q, when, last):
        @pl.when(when)
        def _():
            arrive(("own", q), region(q, mine))
            for key, target in (("psi_y", to_y), ("psi_c", to_c)):
                i = slot((key, q))
                remote(i, i, region(q, mine), region(q, mine), target).start()
        if last:
            spread_reg(q)

    stays_up = jnp.logical_and(x == 1, core == 1)

    def spread_reg(q):
        if True:
            for key, target in (("psi_y", to_y), ("psi_c", to_c)):
                i = slot((key, q))
                started[(key, q)] = [(remote(i, i, region(q, mine), region(q, mine), target), None)]
                lands[(key, q)] = region(q, mine)

    def relay(q):
        arrive(("psi_y", q), region(q, across))
        send(("psi_yc", q), region(q, across), region(q, across), to_c)

    def complete(q):
        arrive(("psi_c", q), region(q, mates))
        arrive(("psi_yc", q), region(q, corner))


    @pl.when(moves)
    def _():
        for p in range(phys):
            arrive(("site", p), site.at[pieces[p], block(mine), :])
            src = site.at[pieces[p], block(mine), :]
            remote(slot(("site_y", p)), slot(("site_y", p)), src, src, to_y).start()
            remote(slot(("site_c", p)), slot(("site_c", p)), src, src, to_c).start()

    @pl.when(stays)
    def _():
        for p in range(phys):
            arrive(("site", p), site.at[pieces[p], block(mine), :])

    for p in range(phys):
        for key, target in (("site_y", to_y), ("site_c", to_c)):
            src = site.at[pieces[p], block(mine), :]
            i = slot((key, p))
            started[(key, p)] = [(remote(i, i, src, src, target), None)]

    loads["mpo"].wait()

    def iota(shape, axis):
        return lax.broadcasted_iota(jnp.int32, shape, axis)

    def one_hot(condition):
        return jnp.where(condition, 1.0, 0.0).astype(BF16)

    small = phys * width
    codes = width * pq
    flat = mpo_raw[...].astype(F32).reshape(codes, width).astype(BF16)
    spread_n = one_hot(lax.rem(iota((width, small), 1), width) == iota((width, small), 0))
    same_u = lax.rem(iota((codes, small), 0), phys) == lax.div(iota((codes, small), 1), width)
    tall_un = jnp.where(same_u, mm(flat, spread_n), 0.0).astype(BF16)
    code = iota((codes, small), 0)
    code_sm = lax.rem(lax.div(code, phys), phys) * width + lax.div(code, pq)
    pick_sm = one_hot(code_sm == iota((codes, small), 1))
    over_codes = (((0,), (0,)), ((), ()))
    mpo[...] = lax.dot_general(tall_un, pick_sm, over_codes, preferred_element_type=F32).astype(BF16)
    big = small * group
    tall_code = lax.div(iota((big, small), 0), group)
    spread_rows = one_hot(tall_code == iota((big, small), 1))
    col = iota((small, big), 1)
    col_code = lax.div(col, group * width) * width + lax.rem(col, width)
    spread_cols = one_hot(col_code == iota((small, big), 0))
    wide = mm(mm(spread_rows, mpo[...]).astype(BF16), spread_cols)
    same = lax.rem(iota((big, big), 0), group) == lax.rem(lax.div(iota((big, big), 1), width), group)
    mix[...] = jnp.where(same, wide, 0.0).astype(BF16)

    for t in range(phys):
        own = site[t, block(mine), :].astype(F32)
        for i in range(cuts):
            tile = own[:, i * lanes:(i + 1) * lanes]
            site_tr[i * lanes:(i + 1) * lanes, t * rows:(t + 1) * rows] = tile.T.astype(BF16)

    spread_if(0, stays, False)
    for p in range(phys):
        arrive(("site_y", p), site.at[pieces[p], block(across), :])
        send(("site_yc", p), site.at[pieces[p], block(across), :], site.at[pieces[p], block(across), :], to_c)

    spread_if(1, psi_self, False)
    for p in range(phys):
        arrive(("site_c", p), site.at[pieces[p], block(mates), :])
        arrive(("site_yc", p), site.at[pieces[p], block(corner), :])

    send(("right",), right_h, right, to_c, when=moves)
    keep(("right",), right_h, right, moves)
    strip = group * width
    per_left = tall_left // group

    for i in range(n_left):
        arrive(("left", i), left.at[left_part(i)])

        @pl.loop(i * per_left, (i + 1) * per_left, unroll=per_left)
        def _(g):
            ours = left[pl.ds(pl.multiple_of(g * group, group), group)].astype(F32)
            ours = ours.reshape(strip, chi).astype(BF16)
            first = jnp.concatenate([mm(ours, site[s]).astype(BF16) for s in range(phys)], axis=0)
            out = mm(mix[...], first).astype(BF16)
            for u in range(phys):
                for n in range(width):
                    at = (u * width + n) * group
                    where = pl.multiple_of(u * rows + g * group, group)
                    second[n, pl.ds(where, group), :] = out[at:at + group, :]

        if i == 0:
            spread_if(1, stays_up, False)
        if i == n_left - 2:
            pl.when(jnp.logical_and(psi_waits, z == top))(lambda: pl.semaphore_wait(chain.at[1], 1))
            for q in range(cuts):
                launch_late(q)
            spread_if(2, stays, False)


    hrows = rows // 2

    def rows_of(stage, far, half):
        yy = 1 - y if far else y
        column = 1 - x if stage == 0 else x
        start = (2 * yy + column) * rows + half * hrows
        return pl.ds(pl.multiple_of(start, hrows), hrows)

    def block_of(stage, far):
        yy = 1 - y if far else y
        column = 1 - x if stage == 0 else x
        return block(2 * yy + column)

    def partial(stage):
        for far in (1, 0):
            where = block_of(stage, far)
            for n in range(width):
                part[n, where, :] = mm(site_tr[where, :], second[n]).astype(BF16)

    def swap_halves(stage):
        for far in (1, 0):
            send(("rs1", stage, far), part.at[:, rows_of(stage, far, 1 - core), :], rs1.at[stage, far], to_c)

    n_rs = 4
    rs_rows = hrows // n_rs

    def add_far(stage):
        arrive(("rs1", stage, 1), rs1.at[stage, 1])
        for n in range(width):
            total = part[n, rows_of(stage, 1, core), :].astype(F32) + rs1[stage, 1, n].astype(F32)
            send2[stage, n] = total.astype(BF16)

    def send_far(stage, when=None):
        for j in range(n_rs):
            where = pl.ds(j * rs_rows, rs_rows)
            send(("rs2", stage, j), send2.at[stage, :, where, :], rs2.at[stage, :, where, :], to_y, when=when)

    def finish(stage, parts):
        if parts[0] == 0:
            arrive(("rs1", stage, 0), rs1.at[stage, 0])
        base = stage * hrows * width
        for j in parts:
            where = pl.ds(j * rs_rows, rs_rows)
            arrive(("rs2", stage, j), rs2.at[stage, :, where, :])
            yy = y
            column = 1 - x if stage == 0 else x
            start = (2 * yy + column) * rows + core * hrows + j * rs_rows
            near = pl.ds(pl.multiple_of(start, rs_rows), rs_rows)
            for n in range(width):
                total = part[n, near, :].astype(F32) + rs1[stage, 0, n, where, :].astype(F32)
                total += rs2[stage, n, where, :].astype(F32)
                for i in range(cuts):
                    acc[i, pl.ds(base + j * rs_rows * width + n, rs_rows, stride=width), :] = (
                        total[:, i * lanes:(i + 1) * lanes])
            high = pl.ds(j * rs_rows * width, rs_rows * width)
            whole = jnp.concatenate(
                [acc[i, pl.ds(base + j * rs_rows * width, rs_rows * width), :] for i in range(cuts)], axis=1)
            nl_own[stage, high, :] = whole.astype(BF16)
            nl_out[stage, where] = whole.reshape(rs_rows, width, chi).astype(BF16)
            send(("up", stage, j), nl_own.at[stage, high, :], nl_in.at[stage, high, :], to_up, when=shifts)
            keep(("up", stage, j), nl_own.at[stage, high, :], nl_in.at[stage, high, :], rests)

    my_half = pl.ds(pl.multiple_of(core * hrows, hrows), hrows)
    mate_half = pl.ds(pl.multiple_of((1 - core) * hrows, hrows), hrows)
    nl_slots = [slot(("nl_land", h)) for h in range(2)]
    assert nl_slots[1] == nl_slots[0] + 1
    nl_land = nl_slots[0] + core
    n_out = 4
    out_slots = [[slot(("out_land", h, j)) for j in range(n_out)] for h in range(2)]
    out_rows = hrows // n_out

    def home_left(stage):
        src, dst = nl_out.at[stage], new_left.at[my_half]
        if stage == 0:
            send(("nl0", 0), src, dst, to_x, when=stays, land=nl_land)
            send(("nl0", 1), src, dst, to_xc, when=moves, land=nl_land)
        else:
            send(("nl1", 0), src, dst, to_c, when=moves, land=nl_land)
            keep(("nl1", 1), src, dst, stays, land=nl_land)

    def home_product(stage, j):
        start = core * hrows + j * out_rows
        dst = product.at[pl.ds(pl.multiple_of(start, out_rows), out_rows)]
        src = prod.at[stage, pl.ds(j * out_rows, out_rows)]
        land = out_slots[0][j] + core * n_out
        if stage == 0:
            send(("out0", j, 0), src, dst, to_xc, when=stays, land=land)
            send(("out0", j, 1), src, dst, to_x, when=moves, land=land)
        else:
            send(("out1", j, 0), src, dst, to_c, when=stays, land=land)
            keep(("out1", j, 1), src, dst, moves, land=land)

    def finalize():
        for key in list(started):
            if key[0] not in ("nl0", "nl1", "out0", "out1") and key not in landed:
                arrive(key, lands[key])
        for h in range(2):
            where = pl.ds(h * hrows, hrows)
            for stage, when in ((0, moves), (1, stays)):
                if (f"nl{stage}", 0) in started:
                    pl.when(when)(functools.partial(arrive, ("nl_land", h), new_left.at[where]))
            for stage, when in ((0, stays), (1, moves)):
                for j in range(n_out):
                    if (f"out{stage}", j, 0) in started:
                        where = pl.ds(h * hrows + j * out_rows, out_rows)
                        pl.when(when)(functools.partial(arrive, ("out_land", h, j), product.at[where]))
        for copies in started.values():
            for copy, when in copies:
                if when is None:
                    copy.wait_send()
                else:
                    pl.when(when)(copy.wait_send)

    partial(0)
    swap_halves(0)
    partial(1)
    add_far(0)
    swap_halves(1)
    send_far(0)
    spread_if(0, moves, True)

    side = width * pq
    col = iota((small, side), 1)
    col_m = lax.rem(col, width)
    col_sv = lax.rem(lax.div(col, width), pq // 2) * 2 + lax.div(col, width * (pq // 2))
    col_s, col_v = lax.div(col_sv, phys), lax.rem(col_sv, phys)
    row = iota((side, small), 0)
    row_k, row_u, row_w = lax.div(row, pq), lax.rem(lax.div(row, phys), phys), lax.rem(row, phys)
    code_c, code_r = iota((small, side), 0), iota((side, small), 1)
    t1 = mm(mpo[...], one_hot(col_s * width + col_m == code_c)).astype(BF16)
    t2 = mm(one_hot(row_w * width + row_k == code_r), mpo[...]).astype(BF16)
    both = jnp.zeros((side, side), F32)
    for n in range(width):
        near = mm(one_hot(row_u * width + n == code_r), t1)
        both += near * mm(t2, one_hot(col_v * width + n == code_c))
    pair[...] = both.astype(BF16)

    add_far(1)
    spread_if(1, moves, True)
    finish(0, range(n_rs))
    home_left(0)
    spread_if(2, moves, False)
    relay(0)
    arrive(("right",), right)
    for i in range(cuts):
        acc[i, batch * pq:2 * batch * pq, :] = jnp.zeros((batch * pq, lanes), F32)

    def contract(stage, q, lo, n):
        ours = nl_in[stage, lo * width:(lo + n) * width, :]
        for t in range(pq // 2):
            mixed[t, :n * width, :] = mm(ours, psi[q, t])

    def project(p):
        here = mixed[:, p * 2 * width:(p + 1) * 2 * width, :]
        tiles = []
        for i in range(2):
            one = here[:, i * width:(i + 1) * width, :].reshape(pq // 2 * width, 2 * lanes)
            tiles.append(jnp.concatenate([one[:, :lanes], one[:, lanes:]], axis=0))
        both = jnp.concatenate(tiles, axis=1).astype(BF16)
        out = mm(pair[...], both).astype(BF16)
        for i in range(2):
            where = pl.ds((p * 2 + i) * pq, pq)
            for k in range(width):
                proj[where, k * lanes:(k + 1) * lanes] = out[k * pq:(k + 1) * pq, i * lanes:(i + 1) * lanes]

    def environment(q):
        start = q * lanes if isinstance(q, int) else pl.multiple_of(q * lanes, lanes)
        return right[:, pl.ds(start, lanes), :].reshape(width * lanes, chi)

    def gathered(where):
        return jnp.concatenate([acc[i, where, :] for i in range(cuts)], axis=1)

    def strip_of(stage, q, lo=0, n=None):
        n = batch if n is None else n
        contract(stage, q, lo, n)
        for p in range(n // 2):
            project(p)
        total = mm(proj[:n * pq, :], environment(q))
        where = pl.ds((stage * batch + lo) * pq, n * pq)
        if not isinstance(q, int) or q > 0:
            total += gathered(where)
        for i in range(cuts):
            acc[i, where, :] = total[:, i * lanes:(i + 1) * lanes]

    def last_strip(stage, lo=0, n=None):
        n = batch if n is None else n
        q = cuts - 1
        contract(stage, q, lo, n)
        high = out_rows * pq
        for j in range(n // out_rows):
            for p in range(out_rows // 2):
                project(j * (out_rows // 2) + p)
            total = mm(proj[j * high:(j + 1) * high, :], environment(q))
            total += gathered(pl.ds((stage * batch + lo) * pq + j * high, high))
            out = total.reshape(out_rows, phys, phys, chi).astype(BF16)
            prod[stage, lo + j * out_rows:lo + (j + 1) * out_rows] = out
            home_product(stage, lo // out_rows + j)

    complete(0)
    spread_if(3, moves, False)
    for j in range(n_rs):
        high = pl.ds(j * rs_rows * width, rs_rows * width)
        arrive(("up", 0, j), nl_in.at[0, high, :])
    strip_of(0, 0)
    relay(1)
    complete(1)
    spread_if(3, stays, False)
    spread_reg(2)
    spread_reg(3)
    strip_of(0, 1)
    relay(2)
    complete(2)
    strip_of(0, 2)
    send_far(1, moves)
    relay(3)
    complete(3)
    send_far(1, stays)
    last_strip(0)
    def landed_rows(stage, parts):
        for j in parts:
            high = pl.ds(j * rs_rows * width, rs_rows * width)
            arrive(("up", stage, j), nl_in.at[stage, high, :])

    few = batch // 2
    early_parts, late_parts = range(n_rs // 2), range(n_rs // 2, n_rs)
    finish(1, early_parts)
    landed_rows(1, early_parts)

    strip_of(1, 0, 0, few)

    finish(1, late_parts)
    home_left(1)
    @pl.loop(1, cuts - 1)
    def _(q):
        strip_of(1, q, 0, few)

    last_strip(1, 0, few)
    landed_rows(1, late_parts)

    @pl.loop(0, cuts - 1)
    def _(q):
        strip_of(1, q, few, few)

    last_strip(1, few, few)
    finalize()


def fused(left_env, site, psi, right_env, mpo):
    _, rows, width, chi = left_env.shape
    phys = site.shape[2]
    pq = phys * phys
    group, cuts, batch = 16, 4, rows // 2
    lanes = chi // cuts
    small = phys * width
    table = mpo.transpose(0, 2, 3, 1)
    n_sems = 120
    any_spec = pl.BlockSpec(memory_space=pl.ANY)
    new_left, product = pl.pallas_call(
        functools.partial(kernel, (rows, width, phys, chi, group, cuts, batch)),
        out_shape=(
            jax.ShapeDtypeStruct((rows, width, chi), BF16),
            jax.ShapeDtypeStruct((rows, phys, phys, chi), BF16),
        ),
        in_specs=[any_spec] * 5,
        out_specs=(any_spec, any_spec),
        scratch_shapes=[
            pltpu.VMEM((rows, width, chi), BF16),
            pltpu.VMEM((rows, phys, chi), BF16),
            pltpu.VMEM((rows, phys, phys, chi), BF16),
            pltpu.VMEM((width, phys, phys, width), BF16),
            pltpu.VMEM((small, small), BF16),
            pltpu.VMEM((width, chi, chi), BF16),
            pltpu.VMEM((phys, rows, chi), BF16),
            pltpu.VMEM((cuts, pq // 2, rows, 2 * lanes), BF16),
            pltpu.VMEM((phys, chi, chi), BF16),
            pltpu.VMEM((chi, phys * rows), BF16),
            pltpu.VMEM((small * group, small * group), BF16),
            pltpu.VMEM((width * pq, width * pq), BF16),
            pltpu.VMEM((width, phys * rows, chi), BF16),
            pltpu.VMEM((width, chi, chi), BF16),
            pltpu.VMEM((2, 2, width, rows // 2, chi), BF16),
            pltpu.VMEM((2, width, rows // 2, chi), BF16),
            pltpu.VMEM((2, width, rows // 2, chi), BF16),
            pltpu.VMEM((2, rows // 2 * width, chi), BF16),
            pltpu.VMEM((2, rows // 2, width, chi), BF16),
            pltpu.VMEM((2, rows // 2 * width, chi), BF16),
            pltpu.VMEM((cuts, pq // 2, chi, 2 * lanes), BF16),
            pltpu.VMEM((pq // 2, batch * width, 2 * lanes), F32),
            pltpu.VMEM((batch * pq, width * lanes), BF16),
            pltpu.VMEM((2, rows // 2, phys, phys, chi), BF16),
            pltpu.VMEM((cuts, rows * pq, lanes), F32),
            pltpu.SemaphoreType.DMA((6,)),
            pltpu.SemaphoreType.DMA((n_sems,)),
            pltpu.SemaphoreType.DMA((n_sems,)),
            pltpu.SemaphoreType.REGULAR((2,)),
        ],
        compiler_params=pltpu.CompilerParams(
            collective_id=0, has_side_effects=True, vmem_limit_bytes=62 * 1024 * 1024
        ),
    )(left_env[0], site[0], psi[0], right_env[0], table)
    return new_left[None], product[None]


def shifted(block, axis, distance):
    devices = range(lax.axis_size(axis))
    route = [((i - distance) % len(devices), i) for i in devices]
    return lax.ppermute(block, axis, route)


def shards(left_env, site, psi, right_env, mpo):
    left = left_env[0]
    tensor = site[0]
    rows = tensor.shape[0]
    phys = tensor.shape[1]
    chi = tensor.shape[2]
    width = left.shape[1]
    pair_source = shifted(psi[0], "sec", 1)
    offset = lax.axis_index("bond") * rows
    whole_left, whole_site = (
        lax.all_gather(left, "bond", axis=0, tiled=True),
        lax.all_gather(tensor, "bond", axis=0, tiled=True),
    )
    own_cols = lax.dynamic_slice_in_dim(whole_site, offset, rows, 2)
    first = jnp.dot(
        whole_left.reshape(chi * width, chi),
        own_cols.reshape(chi, phys * rows),
        preferred_element_type=jnp.float32,
    )
    first = first.astype(jnp.bfloat16).reshape(chi, width, phys, rows)
    second = jnp.einsum("pmsb,mnsu->punb", first, mpo, preferred_element_type=jnp.float32).astype(
        jnp.bfloat16
    )
    fresh = lax.dot_general(
        whole_site.reshape(chi * phys, chi),
        second.reshape(chi * phys, width * rows),
        (((0,), (0,)), ((), ())),
        preferred_element_type=jnp.float32,
    )
    fresh = fresh.astype(jnp.bfloat16).reshape(chi, width, rows)
    new_left = lax.all_to_all(fresh, "bond", split_axis=0, concat_axis=2, tiled=True)
    left_source = shifted(new_left, "sec", 1)
    source_flat = left_source.reshape(rows * width, chi)
    pair = pair_source.reshape(rows, phys * phys * chi)
    mixed = jnp.dot(
        source_flat,
        lax.all_gather(pair, "bond", axis=0, tiled=True),
        preferred_element_type=jnp.float32,
    )
    mixed = mixed.astype(jnp.bfloat16).reshape(rows, width * phys * phys, chi)
    two_site = jnp.einsum("mnsu,nkvw->msvuwk", mpo, mpo, preferred_element_type=jnp.float32)
    two_site = two_site.astype(jnp.bfloat16).reshape(width * phys * phys, phys * phys * width)
    projected = jnp.einsum(
        "pqc,qr->prc", mixed, two_site, preferred_element_type=jnp.float32
    ).astype(jnp.bfloat16)
    env_right = right_env[0].reshape(width * chi, chi)
    result = jnp.dot(
        projected.reshape(rows * phys * phys, width * chi),
        env_right,
        preferred_element_type=jnp.float32,
    ).astype(jnp.bfloat16)
    return (new_left[None], result.reshape(1, rows, phys, phys, chi))


def solution(mesh):
    in_specs = (
        P("sec", "bond", None, None),
        P("sec", "bond", None, None),
        P("sec", "bond", None, None, None),
        P("sec", None, None, None),
        P(),
    )
    out_specs = (P("sec", "bond", None, None), P("sec", "bond", None, None, None))
    body = fused if mesh.shape["bond"] == 4 else shards
    return jax.shard_map(body, mesh=mesh, in_specs=in_specs, out_specs=out_specs, check_vma=False)
```

```python
import functools

import jax
import jax.numpy as jnp
from jax import lax
from jax.experimental import pallas as pl
from jax.experimental.pallas import tpu as pltpu
from jax.sharding import PartitionSpec as P

MESH = pl.DeviceIdType.MESH
BF16 = jnp.bfloat16
F32 = jnp.float32


def mm(a, b):
    return jnp.dot(a, b, preferred_element_type=F32)


def kernel(
    dims,
    left_h, site_h, psi_h, right_h, mpo_h,
    new_left, product,
    left, site_raw, psi_raw, mpo_raw, mpo, right,
    site_own, psi_own, site, site_tr, mix, pair,
    second, part, rs1, send2, rs2, nl_own, nl_out, nl_in, psi, mixed, proj, prod, acc,
    local_sem, send_sem, recv_sem, chain,
):
    rows, width, phys, chi, group, cuts, batch = dims
    pq = phys * phys
    n_sec = lax.axis_size("sec")
    sec = lax.axis_index("sec")
    me = lax.axis_index("bond")
    x, y = lax.rem(me, 2), me // 2
    core, z = lax.rem(sec, 2), sec // 2
    mate_sec = 2 * z + 1 - core
    side_bond = 2 * y + 1 - x
    to_c = {"sec": mate_sec}
    to_y = {"bond": 2 * (1 - y) + x}
    to_x = {"bond": side_bond}
    to_xc = {"sec": mate_sec, "bond": side_bond}
    up = lax.rem(sec + 2, n_sec)
    to_up = {"sec": up}
    stays = x == core
    moves = x != core
    shifts = x == 1
    rests = x == 0

    mine = 2 * y + core
    mates = 2 * y + 1 - core
    across = 2 * (1 - y) + core
    corner = 2 * (1 - y) + 1 - core

    def block(owner):
        return pl.ds(pl.multiple_of(owner * rows, rows), rows)

    loads = {}
    for i, (name, src, dst) in enumerate((
        ("site", site_h, site_raw),
        ("psi", psi_h, psi_raw),
        ("mpo", mpo_h, mpo_raw),
    )):
        loads[name] = pltpu.make_async_copy(src, dst, local_sem.at[i])
        loads[name].start()

    barrier = pltpu.get_barrier_semaphore()
    greeted = [to_c, to_y, to_x, to_xc]
    for target in greeted:
        pl.semaphore_signal(barrier, inc=1, device_id=target, device_id_type=MESH)
    top = n_sec // 2 - 1
    down = lax.rem(sec + n_sec - 2, n_sec)
    down_xc = {"sec": lax.rem(mate_sec + n_sec - 2, n_sec), "bond": side_bond}

    def tell(semaphore, target):
        pl.semaphore_signal(semaphore, inc=1, device_id=target, device_id_type=MESH)

    pl.when(jnp.logical_and(x == 1, z > 0))(lambda: tell(barrier, {"sec": down}))
    pl.when(jnp.logical_and(jnp.logical_and(x == 1, core == 0), z > 0))(lambda: tell(barrier, down_xc))
    climbs = jnp.logical_or(x == 1, core == 1)
    below_top = jnp.logical_and(climbs, z < top)

    lanes = chi // cuts
    loads["site"].wait()
    flat = site_raw[...].astype(F32).reshape(rows * phys, chi)
    for i in range(cuts):
        acc[i, :rows * phys, :] = flat[:, i * lanes:(i + 1) * lanes]
    for t in range(phys):
        for i in range(cuts):
            tile = acc[i, pl.ds(t, rows, stride=phys), :]
            site_own[t, :, i * lanes:(i + 1) * lanes] = tile.astype(BF16)

    started = {}
    counter = {}
    lands = {}
    landed = set()

    def slot(key):
        return counter.setdefault(key, len(counter))

    def remote(i, j, src, dst, target):
        return pltpu.make_async_remote_copy(
            src_ref=src, dst_ref=dst, send_sem=send_sem.at[i], recv_sem=recv_sem.at[j],
            device_id=target, device_id_type=MESH,
        )

    def send(key, src, dst, target, when=None, land=None):
        i = slot(key)
        copy = remote(i, i if land is None else land, src, dst, target)
        if when is None:
            copy.start()
        else:
            pl.when(when)(copy.start)
        started.setdefault(key, []).append((copy, when))
        lands[key] = dst

    def keep(key, src, dst, when, land=None):
        copy = pltpu.make_async_copy(src, dst, recv_sem.at[slot(key) if land is None else land])
        pl.when(when)(copy.start)

    def arrive(key, dst):
        i = slot(key)
        landed.add(key)
        remote(i, i, dst, dst, to_c).wait_recv()

    pieces = tuple(pl.ds(t, 1) for t in range(phys))
    n_left = 4
    tall_left = rows // n_left

    def left_part(i):
        return pl.ds(i * tall_left, tall_left)

    def send_left(i):
        send(("left", i), left_h.at[left_part(i)], left.at[left_part(i)], to_xc, when=moves)
        keep(("left", i), left_h.at[left_part(i)], left.at[left_part(i)], stays)

    pl.semaphore_wait(barrier, len(greeted) + jnp.where(below_top, 1, 0))
    pl.when(jnp.logical_and(x == 1, z == 0))(lambda: tell(chain.at[0], {"sec": up}))

    def site_spread(p, from_own):
        src = site_own.at[pieces[p]] if from_own else site.at[pieces[p], block(mine), :]
        when = stays if from_own else None
        send(("site_y", p), src, site.at[pieces[p], block(mine), :], to_y, when)
        send(("site_c", p), src, site.at[pieces[p], block(mine), :], to_c, when)

    for p in range(phys):
        send(("site", p), site_own.at[pieces[p]], site.at[pieces[p], block(me), :], to_xc, when=moves)
        keep(("site", p), site_own.at[pieces[p]], site.at[pieces[p], block(me), :], stays)
        site_spread(p, True)
    for i in range(n_left):
        send_left(i)


    @pl.when(jnp.logical_and(x == 1, jnp.logical_and(z > 0, z < top)))
    def _():
        pl.semaphore_wait(chain.at[0], 1)
        tell(chain.at[0], {"sec": up})

    loads["psi"].wait()
    tall = 8

    @pl.loop(0, rows // tall)
    def _(g):
        flat = psi_raw[pl.ds(pl.multiple_of(g * tall, tall), tall)].astype(F32)
        flat = flat.reshape(tall * pq, chi)
        where = pl.ds(pl.multiple_of(g * tall * pq, tall * pq), tall * pq)
        for i in range(cuts):
            acc[i, where, :] = flat[:, i * lanes:(i + 1) * lanes]

    def region(q, owner):
        return psi.at[q, :, block(owner), :]

    psi_self = jnp.logical_and(x == 0, core == 0)
    to_psi = {
        "sec": lax.rem(2 * z + x + 2 * core, n_sec),
        "bond": 2 * y + core,
    }

    psi_waits = jnp.logical_and(x == 0, core == 1)
    psi_now = x == 1

    def launch(q):
        send(("own", q), psi_own.at[q], region(q, me), to_psi, when=psi_now)
        keep(("own", q), psi_own.at[q], region(q, me), psi_self)

    def launch_late(q):
        send(("own", q), psi_own.at[q], region(q, me), to_psi, when=psi_waits)

    for q in range(cuts):
        for t in range(pq):
            at = (t % 2) * lanes
            tile = acc[q, pl.ds(t, rows, stride=pq), :]
            psi_own[q, t // 2, :, at:at + lanes] = tile.astype(BF16)

    @pl.when(jnp.logical_and(x == 1, z == top))
    def _():
        pl.semaphore_wait(chain.at[0], 1)
        pl.when(core == 0)(lambda: tell(chain.at[1], to_xc))

    for q in range(cuts):
        launch(q)

    def spread_if(q, when, last):
        @pl.when(when)
        def _():
            arrive(("own", q), region(q, mine))
            for key, target in (("psi_y", to_y), ("psi_c", to_c)):
                i = slot((key, q))
                remote(i, i, region(q, mine), region(q, mine), target).start()
        if last:
            spread_reg(q)

    stays_up = jnp.logical_and(x == 1, core == 1)

    def spread_reg(q):
        if True:
            for key, target in (("psi_y", to_y), ("psi_c", to_c)):
                i = slot((key, q))
                started[(key, q)] = [(remote(i, i, region(q, mine), region(q, mine), target), None)]
                lands[(key, q)] = region(q, mine)

    def relay(q):
        arrive(("psi_y", q), region(q, across))
        send(("psi_yc", q), region(q, across), region(q, across), to_c)

    def complete(q):
        arrive(("psi_c", q), region(q, mates))
        arrive(("psi_yc", q), region(q, corner))


    @pl.when(moves)
    def _():
        for p in range(phys):
            arrive(("site", p), site.at[pieces[p], block(mine), :])
            src = site.at[pieces[p], block(mine), :]
            remote(slot(("site_y", p)), slot(("site_y", p)), src, src, to_y).start()
            remote(slot(("site_c", p)), slot(("site_c", p)), src, src, to_c).start()

    @pl.when(stays)
    def _():
        for p in range(phys):
            arrive(("site", p), site.at[pieces[p], block(mine), :])

    for p in range(phys):
        for key, target in (("site_y", to_y), ("site_c", to_c)):
            src = site.at[pieces[p], block(mine), :]
            i = slot((key, p))
            started[(key, p)] = [(remote(i, i, src, src, target), None)]

    loads["mpo"].wait()

    def iota(shape, axis):
        return lax.broadcasted_iota(jnp.int32, shape, axis)

    def one_hot(condition):
        return jnp.where(condition, 1.0, 0.0).astype(BF16)

    small = phys * width
    codes = width * pq
    flat = mpo_raw[...].astype(F32).reshape(codes, width).astype(BF16)
    spread_n = one_hot(lax.rem(iota((width, small), 1), width) == iota((width, small), 0))
    same_u = lax.rem(iota((codes, small), 0), phys) == lax.div(iota((codes, small), 1), width)
    tall_un = jnp.where(same_u, mm(flat, spread_n), 0.0).astype(BF16)
    code = iota((codes, small), 0)
    code_sm = lax.rem(lax.div(code, phys), phys) * width + lax.div(code, pq)
    pick_sm = one_hot(code_sm == iota((codes, small), 1))
    over_codes = (((0,), (0,)), ((), ()))
    mpo[...] = lax.dot_general(tall_un, pick_sm, over_codes, preferred_element_type=F32).astype(BF16)
    big = small * group
    tall_code = lax.div(iota((big, small), 0), group)
    spread_rows = one_hot(tall_code == iota((big, small), 1))
    col = iota((small, big), 1)
    col_code = lax.div(col, group * width) * width + lax.rem(col, width)
    spread_cols = one_hot(col_code == iota((small, big), 0))
    wide = mm(mm(spread_rows, mpo[...]).astype(BF16), spread_cols)
    same = lax.rem(iota((big, big), 0), group) == lax.rem(lax.div(iota((big, big), 1), width), group)
    mix[...] = jnp.where(same, wide, 0.0).astype(BF16)

    for t in range(phys):
        own = site[t, block(mine), :].astype(F32)
        for i in range(cuts):
            tile = own[:, i * lanes:(i + 1) * lanes]
            site_tr[i * lanes:(i + 1) * lanes, t * rows:(t + 1) * rows] = tile.T.astype(BF16)

    spread_if(0, stays, False)
    for p in range(phys):
        arrive(("site_y", p), site.at[pieces[p], block(across), :])
        send(("site_yc", p), site.at[pieces[p], block(across), :], site.at[pieces[p], block(across), :], to_c)

    spread_if(1, psi_self, False)
    for p in range(phys):
        arrive(("site_c", p), site.at[pieces[p], block(mates), :])
        arrive(("site_yc", p), site.at[pieces[p], block(corner), :])

    send(("right",), right_h, right, to_c, when=moves)
    keep(("right",), right_h, right, moves)
    strip = group * width
    per_left = tall_left // group

    for i in range(n_left):
        arrive(("left", i), left.at[left_part(i)])

        @pl.loop(i * per_left, (i + 1) * per_left, unroll=per_left)
        def _(g):
            ours = left[pl.ds(pl.multiple_of(g * group, group), group)].astype(F32)
            ours = ours.reshape(strip, chi).astype(BF16)
            first = jnp.concatenate([mm(ours, site[s]).astype(BF16) for s in range(phys)], axis=0)
            out = mm(mix[...], first).astype(BF16)
            for u in range(phys):
                for n in range(width):
                    at = (u * width + n) * group
                    where = pl.multiple_of(u * rows + g * group, group)
                    second[n, pl.ds(where, group), :] = out[at:at + group, :]

        if i == 0:
            spread_if(1, stays_up, False)
        if i == n_left - 2:
            pl.when(jnp.logical_and(psi_waits, z == top))(lambda: pl.semaphore_wait(chain.at[1], 1))
            for q in range(cuts):
                launch_late(q)
            spread_if(2, stays, False)


    hrows = rows // 2

    def rows_of(stage, far, half):
        yy = 1 - y if far else y
        column = 1 - x if stage == 0 else x
        start = (2 * yy + column) * rows + half * hrows
        return pl.ds(pl.multiple_of(start, hrows), hrows)

    def block_of(stage, far):
        yy = 1 - y if far else y
        column = 1 - x if stage == 0 else x
        return block(2 * yy + column)

    def partial(stage):
        for far in (1, 0):
            where = block_of(stage, far)
            for n in range(width):
                part[n, where, :] = mm(site_tr[where, :], second[n]).astype(BF16)

    def swap_halves(stage):
        for far in (1, 0):
            send(("rs1", stage, far), part.at[:, rows_of(stage, far, 1 - core), :], rs1.at[stage, far], to_c)

    n_rs = 4
    rs_rows = hrows // n_rs

    def add_far(stage):
        arrive(("rs1", stage, 1), rs1.at[stage, 1])
        for n in range(width):
            total = part[n, rows_of(stage, 1, core), :].astype(F32) + rs1[stage, 1, n].astype(F32)
            send2[stage, n] = total.astype(BF16)

    def send_far(stage, when=None):
        for j in range(n_rs):
            where = pl.ds(j * rs_rows, rs_rows)
            send(("rs2", stage, j), send2.at[stage, :, where, :], rs2.at[stage, :, where, :], to_y, when=when)

    def finish(stage, parts):
        if parts[0] == 0:
            arrive(("rs1", stage, 0), rs1.at[stage, 0])
        base = stage * hrows * width
        for j in parts:
            where = pl.ds(j * rs_rows, rs_rows)
            arrive(("rs2", stage, j), rs2.at[stage, :, where, :])
            yy = y
            column = 1 - x if stage == 0 else x
            start = (2 * yy + column) * rows + core * hrows + j * rs_rows
            near = pl.ds(pl.multiple_of(start, rs_rows), rs_rows)
            for n in range(width):
                total = part[n, near, :].astype(F32) + rs1[stage, 0, n, where, :].astype(F32)
                total += rs2[stage, n, where, :].astype(F32)
                for i in range(cuts):
                    acc[i, pl.ds(base + j * rs_rows * width + n, rs_rows, stride=width), :] = (
                        total[:, i * lanes:(i + 1) * lanes])
            high = pl.ds(j * rs_rows * width, rs_rows * width)
            whole = jnp.concatenate(
                [acc[i, pl.ds(base + j * rs_rows * width, rs_rows * width), :] for i in range(cuts)], axis=1)
            nl_own[stage, high, :] = whole.astype(BF16)
            nl_out[stage, where] = whole.reshape(rs_rows, width, chi).astype(BF16)
            send(("up", stage, j), nl_own.at[stage, high, :], nl_in.at[stage, high, :], to_up, when=shifts)
            keep(("up", stage, j), nl_own.at[stage, high, :], nl_in.at[stage, high, :], rests)

    my_half = pl.ds(pl.multiple_of(core * hrows, hrows), hrows)
    mate_half = pl.ds(pl.multiple_of((1 - core) * hrows, hrows), hrows)
    nl_slots = [slot(("nl_land", h)) for h in range(2)]
    assert nl_slots[1] == nl_slots[0] + 1
    nl_land = nl_slots[0] + core
    n_out = 4
    out_slots = [[slot(("out_land", h, j)) for j in range(n_out)] for h in range(2)]
    out_rows = hrows // n_out

    def home_left(stage):
        src, dst = nl_out.at[stage], new_left.at[my_half]
        if stage == 0:
            send(("nl0", 0), src, dst, to_x, when=stays, land=nl_land)
            send(("nl0", 1), src, dst, to_xc, when=moves, land=nl_land)
        else:
            send(("nl1", 0), src, dst, to_c, when=moves, land=nl_land)
            keep(("nl1", 1), src, dst, stays, land=nl_land)

    def home_product(stage, j):
        start = core * hrows + j * out_rows
        dst = product.at[pl.ds(pl.multiple_of(start, out_rows), out_rows)]
        src = prod.at[stage, pl.ds(j * out_rows, out_rows)]
        land = out_slots[0][j] + core * n_out
        if stage == 0:
            send(("out0", j, 0), src, dst, to_xc, when=stays, land=land)
            send(("out0", j, 1), src, dst, to_x, when=moves, land=land)
        else:
            send(("out1", j, 0), src, dst, to_c, when=stays, land=land)
            keep(("out1", j, 1), src, dst, moves, land=land)

    def finalize():
        for key in list(started):
            if key[0] not in ("nl0", "nl1", "out0", "out1") and key not in landed:
                arrive(key, lands[key])
        for h in range(2):
            where = pl.ds(h * hrows, hrows)
            for stage, when in ((0, moves), (1, stays)):
                if (f"nl{stage}", 0) in started:
                    pl.when(when)(functools.partial(arrive, ("nl_land", h), new_left.at[where]))
            for stage, when in ((0, stays), (1, moves)):
                for j in range(n_out):
                    if (f"out{stage}", j, 0) in started:
                        where = pl.ds(h * hrows + j * out_rows, out_rows)
                        pl.when(when)(functools.partial(arrive, ("out_land", h, j), product.at[where]))
        for copies in started.values():
            for copy, when in copies:
                if when is None:
                    copy.wait_send()
                else:
                    pl.when(when)(copy.wait_send)

    partial(0)
    swap_halves(0)
    partial(1)
    add_far(0)
    swap_halves(1)
    send_far(0)
    spread_if(0, moves, True)

    side = width * pq
    col = iota((small, side), 1)
    col_m = lax.rem(col, width)
    col_sv = lax.rem(lax.div(col, width), pq // 2) * 2 + lax.div(col, width * (pq // 2))
    col_s, col_v = lax.div(col_sv, phys), lax.rem(col_sv, phys)
    row = iota((side, small), 0)
    row_k, row_u, row_w = lax.div(row, pq), lax.rem(lax.div(row, phys), phys), lax.rem(row, phys)
    code_c, code_r = iota((small, side), 0), iota((side, small), 1)
    t1 = mm(mpo[...], one_hot(col_s * width + col_m == code_c)).astype(BF16)
    t2 = mm(one_hot(row_w * width + row_k == code_r), mpo[...]).astype(BF16)
    both = jnp.zeros((side, side), F32)
    for n in range(width):
        near = mm(one_hot(row_u * width + n == code_r), t1)
        both += near * mm(t2, one_hot(col_v * width + n == code_c))
    pair[...] = both.astype(BF16)

    add_far(1)
    spread_if(1, moves, True)
    finish(0, range(n_rs))
    home_left(0)
    spread_if(2, moves, False)
    relay(0)
    arrive(("right",), right)
    for i in range(cuts):
        acc[i, batch * pq:2 * batch * pq, :] = jnp.zeros((batch * pq, lanes), F32)

    def contract(stage, q, lo, n):
        ours = nl_in[stage, lo * width:(lo + n) * width, :]
        for t in range(pq // 2):
            mixed[t, :n * width, :] = mm(ours, psi[q, t])

    def project(p):
        here = mixed[:, p * 2 * width:(p + 1) * 2 * width, :]
        tiles = []
        for i in range(2):
            one = here[:, i * width:(i + 1) * width, :].reshape(pq // 2 * width, 2 * lanes)
            tiles.append(jnp.concatenate([one[:, :lanes], one[:, lanes:]], axis=0))
        both = jnp.concatenate(tiles, axis=1).astype(BF16)
        out = mm(pair[...], both).astype(BF16)
        for i in range(2):
            where = pl.ds((p * 2 + i) * pq, pq)
            for k in range(width):
                proj[where, k * lanes:(k + 1) * lanes] = out[k * pq:(k + 1) * pq, i * lanes:(i + 1) * lanes]

    def environment(q):
        start = q * lanes if isinstance(q, int) else pl.multiple_of(q * lanes, lanes)
        return right[:, pl.ds(start, lanes), :].reshape(width * lanes, chi)

    def gathered(where):
        return jnp.concatenate([acc[i, where, :] for i in range(cuts)], axis=1)

    def strip_of(stage, q, lo=0, n=None):
        n = batch if n is None else n
        contract(stage, q, lo, n)
        for p in range(n // 2):
            project(p)
        total = mm(proj[:n * pq, :], environment(q))
        where = pl.ds((stage * batch + lo) * pq, n * pq)
        if not isinstance(q, int) or q > 0:
            total += gathered(where)
        for i in range(cuts):
            acc[i, where, :] = total[:, i * lanes:(i + 1) * lanes]

    def last_strip(stage, lo=0, n=None):
        n = batch if n is None else n
        q = cuts - 1
        contract(stage, q, lo, n)
        high = out_rows * pq
        for j in range(n // out_rows):
            for p in range(out_rows // 2):
                project(j * (out_rows // 2) + p)
            total = mm(proj[j * high:(j + 1) * high, :], environment(q))
            total += gathered(pl.ds((stage * batch + lo) * pq + j * high, high))
            out = total.reshape(out_rows, phys, phys, chi).astype(BF16)
            prod[stage, lo + j * out_rows:lo + (j + 1) * out_rows] = out
            home_product(stage, lo // out_rows + j)

    complete(0)
    spread_if(3, moves, False)
    for j in range(n_rs):
        high = pl.ds(j * rs_rows * width, rs_rows * width)
        arrive(("up", 0, j), nl_in.at[0, high, :])
    strip_of(0, 0)
    relay(1)
    complete(1)
    spread_if(3, stays, False)
    spread_reg(2)
    spread_reg(3)
    strip_of(0, 1)
    relay(2)
    complete(2)
    strip_of(0, 2)
    send_far(1, moves)
    relay(3)
    complete(3)
    send_far(1, stays)
    last_strip(0)
    def landed_rows(stage, parts):
        for j in parts:
            high = pl.ds(j * rs_rows * width, rs_rows * width)
            arrive(("up", stage, j), nl_in.at[stage, high, :])

    few = batch // 2
    early_parts, late_parts = range(n_rs // 2), range(n_rs // 2, n_rs)
    finish(1, early_parts)
    landed_rows(1, early_parts)

    strip_of(1, 0, 0, few)

    finish(1, late_parts)
    home_left(1)
    @pl.loop(1, cuts - 1)
    def _(q):
        strip_of(1, q, 0, few)

    last_strip(1, 0, few)
    landed_rows(1, late_parts)

    @pl.loop(0, cuts - 1)
    def _(q):
        strip_of(1, q, few, few)

    last_strip(1, few, few)
    finalize()


def fused(left_env, site, psi, right_env, mpo):
    _, rows, width, chi = left_env.shape
    phys = site.shape[2]
    pq = phys * phys
    group, cuts, batch = 16, 4, rows // 2
    lanes = chi // cuts
    small = phys * width
    table = mpo.transpose(0, 2, 3, 1)
    n_sems = 120
    any_spec = pl.BlockSpec(memory_space=pl.ANY)
    new_left, product = pl.pallas_call(
        functools.partial(kernel, (rows, width, phys, chi, group, cuts, batch)),
        out_shape=(
            jax.ShapeDtypeStruct((rows, width, chi), BF16),
            jax.ShapeDtypeStruct((rows, phys, phys, chi), BF16),
        ),
        in_specs=[any_spec] * 5,
        out_specs=(any_spec, any_spec),
        scratch_shapes=[
            pltpu.VMEM((rows, width, chi), BF16),
            pltpu.VMEM((rows, phys, chi), BF16),
            pltpu.VMEM((rows, phys, phys, chi), BF16),
            pltpu.VMEM((width, phys, phys, width), BF16),
            pltpu.VMEM((small, small), BF16),
            pltpu.VMEM((width, chi, chi), BF16),
            pltpu.VMEM((phys, rows, chi), BF16),
            pltpu.VMEM((cuts, pq // 2, rows, 2 * lanes), BF16),
            pltpu.VMEM((phys, chi, chi), BF16),
            pltpu.VMEM((chi, phys * rows), BF16),
            pltpu.VMEM((small * group, small * group), BF16),
            pltpu.VMEM((width * pq, width * pq), BF16),
            pltpu.VMEM((width, phys * rows, chi), BF16),
            pltpu.VMEM((width, chi, chi), BF16),
            pltpu.VMEM((2, 2, width, rows // 2, chi), BF16),
            pltpu.VMEM((2, width, rows // 2, chi), BF16),
            pltpu.VMEM((2, width, rows // 2, chi), BF16),
            pltpu.VMEM((2, rows // 2 * width, chi), BF16),
            pltpu.VMEM((2, rows // 2, width, chi), BF16),
            pltpu.VMEM((2, rows // 2 * width, chi), BF16),
            pltpu.VMEM((cuts, pq // 2, chi, 2 * lanes), BF16),
            pltpu.VMEM((pq // 2, batch * width, 2 * lanes), F32),
            pltpu.VMEM((batch * pq, width * lanes), BF16),
            pltpu.VMEM((2, rows // 2, phys, phys, chi), BF16),
            pltpu.VMEM((cuts, rows * pq, lanes), F32),
            pltpu.SemaphoreType.DMA((6,)),
            pltpu.SemaphoreType.DMA((n_sems,)),
            pltpu.SemaphoreType.DMA((n_sems,)),
            pltpu.SemaphoreType.REGULAR((2,)),
        ],
        compiler_params=pltpu.CompilerParams(
            collective_id=0, has_side_effects=True, vmem_limit_bytes=62 * 1024 * 1024
        ),
    )(left_env[0], site[0], psi[0], right_env[0], table)
    return settle(new_left, product)


def settle(*arrays):
    cut = 4

    def body(*refs):
        n = len(arrays)
        srcs, dsts, tmps, sem = refs[:n], refs[n:2 * n], refs[2 * n:3 * n], refs[3 * n]
        moves = []
        for i in reversed(range(n)):
            step = arrays[i].shape[0] // cut
            for j in range(cut):
                part = pl.ds(j * step, step)
                come = pltpu.make_async_copy(srcs[i].at[part], tmps[i].at[part], sem.at[0, i, j])
                go = pltpu.make_async_copy(tmps[i].at[part], dsts[i].at[0, part], sem.at[1, i, j])
                come.start()
                moves.append((come, go))
        for come, go in moves:
            come.wait()
            go.start()
        for _, go in moves:
            go.wait()

    spec = pl.BlockSpec(memory_space=pl.ANY)
    return pl.pallas_call(
        body,
        out_shape=tuple(jax.ShapeDtypeStruct((1,) + a.shape, a.dtype) for a in arrays),
        in_specs=[spec] * len(arrays),
        out_specs=(spec,) * len(arrays),
        scratch_shapes=[pltpu.VMEM(a.shape, a.dtype) for a in arrays]
        + [pltpu.SemaphoreType.DMA((2, len(arrays), cut))],
        compiler_params=pltpu.CompilerParams(vmem_limit_bytes=62 * 1024 * 1024),
    )(*arrays)


def shifted(block, axis, distance):
    devices = range(lax.axis_size(axis))
    route = [((i - distance) % len(devices), i) for i in devices]
    return lax.ppermute(block, axis, route)


def shards(left_env, site, psi, right_env, mpo):
    left = left_env[0]
    tensor = site[0]
    rows = tensor.shape[0]
    phys = tensor.shape[1]
    chi = tensor.shape[2]
    width = left.shape[1]
    pair_source = shifted(psi[0], "sec", 1)
    offset = lax.axis_index("bond") * rows
    whole_left, whole_site = (
        lax.all_gather(left, "bond", axis=0, tiled=True),
        lax.all_gather(tensor, "bond", axis=0, tiled=True),
    )
    own_cols = lax.dynamic_slice_in_dim(whole_site, offset, rows, 2)
    first = jnp.dot(
        whole_left.reshape(chi * width, chi),
        own_cols.reshape(chi, phys * rows),
        preferred_element_type=jnp.float32,
    )
    first = first.astype(jnp.bfloat16).reshape(chi, width, phys, rows)
    second = jnp.einsum("pmsb,mnsu->punb", first, mpo, preferred_element_type=jnp.float32).astype(
        jnp.bfloat16
    )
    fresh = lax.dot_general(
        whole_site.reshape(chi * phys, chi),
        second.reshape(chi * phys, width * rows),
        (((0,), (0,)), ((), ())),
        preferred_element_type=jnp.float32,
    )
    fresh = fresh.astype(jnp.bfloat16).reshape(chi, width, rows)
    new_left = lax.all_to_all(fresh, "bond", split_axis=0, concat_axis=2, tiled=True)
    left_source = shifted(new_left, "sec", 1)
    source_flat = left_source.reshape(rows * width, chi)
    pair = pair_source.reshape(rows, phys * phys * chi)
    mixed = jnp.dot(
        source_flat,
        lax.all_gather(pair, "bond", axis=0, tiled=True),
        preferred_element_type=jnp.float32,
    )
    mixed = mixed.astype(jnp.bfloat16).reshape(rows, width * phys * phys, chi)
    two_site = jnp.einsum("mnsu,nkvw->msvuwk", mpo, mpo, preferred_element_type=jnp.float32)
    two_site = two_site.astype(jnp.bfloat16).reshape(width * phys * phys, phys * phys * width)
    projected = jnp.einsum(
        "pqc,qr->prc", mixed, two_site, preferred_element_type=jnp.float32
    ).astype(jnp.bfloat16)
    env_right = right_env[0].reshape(width * chi, chi)
    result = jnp.dot(
        projected.reshape(rows * phys * phys, width * chi),
        env_right,
        preferred_element_type=jnp.float32,
    ).astype(jnp.bfloat16)
    return (new_left[None], result.reshape(1, rows, phys, phys, chi))


def solution(mesh):
    in_specs = (
        P("sec", "bond", None, None),
        P("sec", "bond", None, None),
        P("sec", "bond", None, None, None),
        P("sec", None, None, None),
        P(),
    )
    out_specs = (P("sec", "bond", None, None), P("sec", "bond", None, None, None))
    body = fused if mesh.shape["bond"] == 4 else shards
    return jax.shard_map(body, mesh=mesh, in_specs=in_specs, out_specs=out_specs, check_vma=False)
```

```python
import functools

import jax
import jax.numpy as jnp
from jax import lax
from jax.experimental import pallas as pl
from jax.experimental.pallas import tpu as pltpu
from jax.sharding import PartitionSpec as P

MESH = pl.DeviceIdType.MESH
BF16 = jnp.bfloat16
F32 = jnp.float32


def mm(a, b):
    return jnp.dot(a, b, preferred_element_type=F32)


def kernel(
    dims,
    left_h, site_h, psi_h, right_h, mpo_h,
    new_left, product,
    left, site_raw, psi_raw, mpo_raw, mpo, right,
    site_own, psi_own, site, site_tr, mix, pair,
    second, part, rs1, send2, rs2, nl_own, nl_out, nl_in, psi, mixed, proj, prod, acc,
    local_sem, send_sem, recv_sem, chain,
):
    rows, width, phys, chi, group, cuts, batch = dims
    pq = phys * phys
    n_sec = lax.axis_size("sec")
    sec = lax.axis_index("sec")
    me = lax.axis_index("bond")
    x, y = lax.rem(me, 2), me // 2
    core, z = lax.rem(sec, 2), sec // 2
    mate_sec = 2 * z + 1 - core
    side_bond = 2 * y + 1 - x
    to_c = {"sec": mate_sec}
    to_y = {"bond": 2 * (1 - y) + x}
    to_x = {"bond": side_bond}
    to_xc = {"sec": mate_sec, "bond": side_bond}
    up = lax.rem(sec + 2, n_sec)
    to_up = {"sec": up}
    stays = x == core
    moves = x != core
    shifts = x == 1
    rests = x == 0

    mine = 2 * y + core
    mates = 2 * y + 1 - core
    across = 2 * (1 - y) + core
    corner = 2 * (1 - y) + 1 - core

    def block(owner):
        return pl.ds(pl.multiple_of(owner * rows, rows), rows)

    loads = {}
    for i, (name, src, dst) in enumerate((
        ("site", site_h, site_raw),
        ("psi", psi_h, psi_raw),
        ("mpo", mpo_h, mpo_raw),
    )):
        loads[name] = pltpu.make_async_copy(src, dst, local_sem.at[i])
        loads[name].start()

    barrier = pltpu.get_barrier_semaphore()
    greeted = [to_c, to_y, to_x, to_xc]
    for target in greeted:
        pl.semaphore_signal(barrier, inc=1, device_id=target, device_id_type=MESH)
    top = n_sec // 2 - 1
    down = lax.rem(sec + n_sec - 2, n_sec)
    down_xc = {"sec": lax.rem(mate_sec + n_sec - 2, n_sec), "bond": side_bond}

    def tell(semaphore, target):
        pl.semaphore_signal(semaphore, inc=1, device_id=target, device_id_type=MESH)

    pl.when(jnp.logical_and(x == 1, z > 0))(lambda: tell(barrier, {"sec": down}))
    pl.when(jnp.logical_and(jnp.logical_and(x == 1, core == 0), z > 0))(lambda: tell(barrier, down_xc))
    climbs = jnp.logical_or(x == 1, core == 1)
    below_top = jnp.logical_and(climbs, z < top)

    lanes = chi // cuts
    loads["site"].wait()
    flat = site_raw[...].astype(F32).reshape(rows * phys, chi)
    for i in range(cuts):
        acc[i, :rows * phys, :] = flat[:, i * lanes:(i + 1) * lanes]
    for t in range(phys):
        for i in range(cuts):
            tile = acc[i, pl.ds(t, rows, stride=phys), :]
            site_own[t, :, i * lanes:(i + 1) * lanes] = tile.astype(BF16)

    started = {}
    counter = {}
    lands = {}
    landed = set()

    def slot(key):
        return counter.setdefault(key, len(counter))

    def remote(i, j, src, dst, target):
        return pltpu.make_async_remote_copy(
            src_ref=src, dst_ref=dst, send_sem=send_sem.at[i], recv_sem=recv_sem.at[j],
            device_id=target, device_id_type=MESH,
        )

    def send(key, src, dst, target, when=None, land=None):
        i = slot(key)
        copy = remote(i, i if land is None else land, src, dst, target)
        if when is None:
            copy.start()
        else:
            pl.when(when)(copy.start)
        started.setdefault(key, []).append((copy, when))
        lands[key] = dst

    def keep(key, src, dst, when, land=None):
        copy = pltpu.make_async_copy(src, dst, recv_sem.at[slot(key) if land is None else land])
        pl.when(when)(copy.start)

    def arrive(key, dst):
        i = slot(key)
        landed.add(key)
        remote(i, i, dst, dst, to_c).wait_recv()

    pieces = tuple(pl.ds(t, 1) for t in range(phys))
    n_left = 4
    tall_left = rows // n_left

    def left_part(i):
        return pl.ds(i * tall_left, tall_left)

    def send_left(i):
        send(("left", i), left_h.at[left_part(i)], left.at[left_part(i)], to_xc, when=moves)
        keep(("left", i), left_h.at[left_part(i)], left.at[left_part(i)], stays)

    pl.semaphore_wait(barrier, len(greeted) + jnp.where(below_top, 1, 0))
    pl.when(jnp.logical_and(x == 1, z == 0))(lambda: tell(chain.at[0], {"sec": up}))

    def site_spread(p, from_own):
        src = site_own.at[pieces[p]] if from_own else site.at[pieces[p], block(mine), :]
        when = stays if from_own else None
        send(("site_y", p), src, site.at[pieces[p], block(mine), :], to_y, when)
        send(("site_c", p), src, site.at[pieces[p], block(mine), :], to_c, when)

    for p in range(phys):
        send(("site", p), site_own.at[pieces[p]], site.at[pieces[p], block(me), :], to_xc, when=moves)
        keep(("site", p), site_own.at[pieces[p]], site.at[pieces[p], block(me), :], stays)
        site_spread(p, True)
    for i in range(n_left):
        send_left(i)


    @pl.when(jnp.logical_and(x == 1, jnp.logical_and(z > 0, z < top)))
    def _():
        pl.semaphore_wait(chain.at[0], 1)
        tell(chain.at[0], {"sec": up})

    loads["psi"].wait()
    tall = 8

    @pl.loop(0, rows // tall)
    def _(g):
        flat = psi_raw[pl.ds(pl.multiple_of(g * tall, tall), tall)].astype(F32)
        flat = flat.reshape(tall * pq, chi)
        where = pl.ds(pl.multiple_of(g * tall * pq, tall * pq), tall * pq)
        for i in range(cuts):
            acc[i, where, :] = flat[:, i * lanes:(i + 1) * lanes]

    def region(q, owner):
        return psi.at[q, :, block(owner), :]

    psi_self = jnp.logical_and(x == 0, core == 0)
    to_psi = {
        "sec": lax.rem(2 * z + x + 2 * core, n_sec),
        "bond": 2 * y + core,
    }

    psi_waits = jnp.logical_and(x == 0, core == 1)
    psi_now = x == 1

    def launch(q):
        send(("own", q), psi_own.at[q], region(q, me), to_psi, when=psi_now)
        keep(("own", q), psi_own.at[q], region(q, me), psi_self)

    def launch_late(q):
        send(("own", q), psi_own.at[q], region(q, me), to_psi, when=psi_waits)

    for q in range(cuts):
        for t in range(pq):
            at = (t % 2) * lanes
            tile = acc[q, pl.ds(t, rows, stride=pq), :]
            psi_own[q, t // 2, :, at:at + lanes] = tile.astype(BF16)

    @pl.when(jnp.logical_and(x == 1, z == top))
    def _():
        pl.semaphore_wait(chain.at[0], 1)
        pl.when(core == 0)(lambda: tell(chain.at[1], to_xc))

    for q in range(cuts):
        launch(q)

    def spread_if(q, when, last):
        @pl.when(when)
        def _():
            arrive(("own", q), region(q, mine))
            for key, target in (("psi_y", to_y), ("psi_c", to_c)):
                i = slot((key, q))
                remote(i, i, region(q, mine), region(q, mine), target).start()
        if last:
            spread_reg(q)

    stays_up = jnp.logical_and(x == 1, core == 1)

    def spread_reg(q):
        if True:
            for key, target in (("psi_y", to_y), ("psi_c", to_c)):
                i = slot((key, q))
                started[(key, q)] = [(remote(i, i, region(q, mine), region(q, mine), target), None)]
                lands[(key, q)] = region(q, mine)

    def relay(q):
        arrive(("psi_y", q), region(q, across))
        send(("psi_yc", q), region(q, across), region(q, across), to_c)

    def complete(q):
        arrive(("psi_c", q), region(q, mates))
        arrive(("psi_yc", q), region(q, corner))


    @pl.when(moves)
    def _():
        for p in range(phys):
            arrive(("site", p), site.at[pieces[p], block(mine), :])
            src = site.at[pieces[p], block(mine), :]
            remote(slot(("site_y", p)), slot(("site_y", p)), src, src, to_y).start()
            remote(slot(("site_c", p)), slot(("site_c", p)), src, src, to_c).start()

    @pl.when(stays)
    def _():
        for p in range(phys):
            arrive(("site", p), site.at[pieces[p], block(mine), :])

    for p in range(phys):
        for key, target in (("site_y", to_y), ("site_c", to_c)):
            src = site.at[pieces[p], block(mine), :]
            i = slot((key, p))
            started[(key, p)] = [(remote(i, i, src, src, target), None)]

    loads["mpo"].wait()

    def iota(shape, axis):
        return lax.broadcasted_iota(jnp.int32, shape, axis)

    def one_hot(condition):
        return jnp.where(condition, 1.0, 0.0).astype(BF16)

    small = phys * width
    codes = width * pq
    flat = mpo_raw[...].astype(F32).reshape(codes, width).astype(BF16)
    spread_n = one_hot(lax.rem(iota((width, small), 1), width) == iota((width, small), 0))
    same_u = lax.rem(iota((codes, small), 0), phys) == lax.div(iota((codes, small), 1), width)
    tall_un = jnp.where(same_u, mm(flat, spread_n), 0.0).astype(BF16)
    code = iota((codes, small), 0)
    code_sm = lax.rem(lax.div(code, phys), phys) * width + lax.div(code, pq)
    pick_sm = one_hot(code_sm == iota((codes, small), 1))
    over_codes = (((0,), (0,)), ((), ()))
    mpo[...] = lax.dot_general(tall_un, pick_sm, over_codes, preferred_element_type=F32).astype(BF16)
    big = small * group
    tall_code = lax.div(iota((big, small), 0), group)
    spread_rows = one_hot(tall_code == iota((big, small), 1))
    col = iota((small, big), 1)
    col_code = lax.div(col, group * width) * width + lax.rem(col, width)
    spread_cols = one_hot(col_code == iota((small, big), 0))
    wide = mm(mm(spread_rows, mpo[...]).astype(BF16), spread_cols)
    same = lax.rem(iota((big, big), 0), group) == lax.rem(lax.div(iota((big, big), 1), width), group)
    mix[...] = jnp.where(same, wide, 0.0).astype(BF16)

    for t in range(phys):
        own = site[t, block(mine), :].astype(F32)
        for i in range(cuts):
            tile = own[:, i * lanes:(i + 1) * lanes]
            site_tr[i * lanes:(i + 1) * lanes, t * rows:(t + 1) * rows] = tile.T.astype(BF16)

    spread_if(0, stays, False)
    for p in range(phys):
        arrive(("site_y", p), site.at[pieces[p], block(across), :])
        send(("site_yc", p), site.at[pieces[p], block(across), :], site.at[pieces[p], block(across), :], to_c)

    spread_if(1, psi_self, False)
    for p in range(phys):
        arrive(("site_c", p), site.at[pieces[p], block(mates), :])
        arrive(("site_yc", p), site.at[pieces[p], block(corner), :])

    send(("right",), right_h, right, to_c, when=moves)
    keep(("right",), right_h, right, moves)
    strip = group * width
    per_left = tall_left // group

    for i in range(n_left):
        arrive(("left", i), left.at[left_part(i)])

        @pl.loop(i * per_left, (i + 1) * per_left, unroll=per_left)
        def _(g):
            ours = left[pl.ds(pl.multiple_of(g * group, group), group)].astype(F32)
            ours = ours.reshape(strip, chi).astype(BF16)
            first = jnp.concatenate([mm(ours, site[s]).astype(BF16) for s in range(phys)], axis=0)
            out = mm(mix[...], first).astype(BF16)
            for u in range(phys):
                for n in range(width):
                    at = (u * width + n) * group
                    where = pl.multiple_of(u * rows + g * group, group)
                    second[n, pl.ds(where, group), :] = out[at:at + group, :]

        if i == 0:
            spread_if(1, stays_up, False)
        if i == n_left - 2:
            pl.when(jnp.logical_and(psi_waits, z == top))(lambda: pl.semaphore_wait(chain.at[1], 1))
            for q in range(cuts):
                launch_late(q)
            spread_if(2, stays, False)


    hrows = rows // 2

    def rows_of(stage, far, half):
        yy = 1 - y if far else y
        column = 1 - x if stage == 0 else x
        start = (2 * yy + column) * rows + half * hrows
        return pl.ds(pl.multiple_of(start, hrows), hrows)

    def block_of(stage, far):
        yy = 1 - y if far else y
        column = 1 - x if stage == 0 else x
        return block(2 * yy + column)

    def partial(stage):
        for far in (1, 0):
            where = block_of(stage, far)
            for n in range(width):
                part[n, where, :] = mm(site_tr[where, :], second[n]).astype(BF16)

    def swap_halves(stage):
        for far in (1, 0):
            send(("rs1", stage, far), part.at[:, rows_of(stage, far, 1 - core), :], rs1.at[stage, far], to_c)

    n_rs = 4
    rs_rows = hrows // n_rs

    def add_far(stage):
        arrive(("rs1", stage, 1), rs1.at[stage, 1])
        for n in range(width):
            total = part[n, rows_of(stage, 1, core), :].astype(F32) + rs1[stage, 1, n].astype(F32)
            send2[stage, n] = total.astype(BF16)

    def send_far(stage, when=None):
        for j in range(n_rs):
            where = pl.ds(j * rs_rows, rs_rows)
            send(("rs2", stage, j), send2.at[stage, :, where, :], rs2.at[stage, :, where, :], to_y, when=when)

    def finish(stage, parts):
        if parts[0] == 0:
            arrive(("rs1", stage, 0), rs1.at[stage, 0])
        base = stage * hrows * width
        for j in parts:
            where = pl.ds(j * rs_rows, rs_rows)
            arrive(("rs2", stage, j), rs2.at[stage, :, where, :])
            yy = y
            column = 1 - x if stage == 0 else x
            start = (2 * yy + column) * rows + core * hrows + j * rs_rows
            near = pl.ds(pl.multiple_of(start, rs_rows), rs_rows)
            for n in range(width):
                total = part[n, near, :].astype(F32) + rs1[stage, 0, n, where, :].astype(F32)
                total += rs2[stage, n, where, :].astype(F32)
                for i in range(cuts):
                    acc[i, pl.ds(base + j * rs_rows * width + n, rs_rows, stride=width), :] = (
                        total[:, i * lanes:(i + 1) * lanes])
            high = pl.ds(j * rs_rows * width, rs_rows * width)
            whole = jnp.concatenate(
                [acc[i, pl.ds(base + j * rs_rows * width, rs_rows * width), :] for i in range(cuts)], axis=1)
            nl_own[stage, high, :] = whole.astype(BF16)
            nl_out[stage, where] = whole.reshape(rs_rows, width, chi).astype(BF16)
            send(("up", stage, j), nl_own.at[stage, high, :], nl_in.at[stage, high, :], to_up, when=shifts)
            keep(("up", stage, j), nl_own.at[stage, high, :], nl_in.at[stage, high, :], rests)

    my_half = pl.ds(pl.multiple_of(core * hrows, hrows), hrows)
    mate_half = pl.ds(pl.multiple_of((1 - core) * hrows, hrows), hrows)
    nl_slots = [slot(("nl_land", h)) for h in range(2)]
    assert nl_slots[1] == nl_slots[0] + 1
    nl_land = nl_slots[0] + core
    n_out = 4
    out_slots = [[slot(("out_land", h, j)) for j in range(n_out)] for h in range(2)]
    out_rows = hrows // n_out

    def home_left(stage):
        src, dst = nl_out.at[stage], new_left.at[my_half]
        if stage == 0:
            send(("nl0", 0), src, dst, to_x, when=stays, land=nl_land)
            send(("nl0", 1), src, dst, to_xc, when=moves, land=nl_land)
        else:
            send(("nl1", 0), src, dst, to_c, when=moves, land=nl_land)
            keep(("nl1", 1), src, dst, stays, land=nl_land)

    def home_product(stage, j):
        start = core * hrows + j * out_rows
        dst = product.at[pl.ds(pl.multiple_of(start, out_rows), out_rows)]
        src = prod.at[stage, pl.ds(j * out_rows, out_rows)]
        land = out_slots[0][j] + core * n_out
        if stage == 0:
            send(("out0", j, 0), src, dst, to_xc, when=stays, land=land)
            send(("out0", j, 1), src, dst, to_x, when=moves, land=land)
        else:
            send(("out1", j, 0), src, dst, to_c, when=stays, land=land)
            keep(("out1", j, 1), src, dst, moves, land=land)

    def finalize():
        for key in list(started):
            if key[0] not in ("nl0", "nl1", "out0", "out1") and key not in landed:
                arrive(key, lands[key])
        for h in range(2):
            where = pl.ds(h * hrows, hrows)
            for stage, when in ((0, moves), (1, stays)):
                if (f"nl{stage}", 0) in started:
                    pl.when(when)(functools.partial(arrive, ("nl_land", h), new_left.at[where]))
            for stage, when in ((0, stays), (1, moves)):
                for j in range(n_out):
                    if (f"out{stage}", j, 0) in started:
                        where = pl.ds(h * hrows + j * out_rows, out_rows)
                        pl.when(when)(functools.partial(arrive, ("out_land", h, j), product.at[where]))
        for copies in started.values():
            for copy, when in copies:
                if when is None:
                    copy.wait_send()
                else:
                    pl.when(when)(copy.wait_send)

    partial(0)
    swap_halves(0)
    partial(1)
    add_far(0)
    swap_halves(1)
    send_far(0)
    spread_if(0, moves, True)

    side = width * pq
    col = iota((small, side), 1)
    col_m = lax.rem(col, width)
    col_sv = lax.rem(lax.div(col, width), pq // 2) * 2 + lax.div(col, width * (pq // 2))
    col_s, col_v = lax.div(col_sv, phys), lax.rem(col_sv, phys)
    row = iota((side, small), 0)
    row_k, row_u, row_w = lax.div(row, pq), lax.rem(lax.div(row, phys), phys), lax.rem(row, phys)
    code_c, code_r = iota((small, side), 0), iota((side, small), 1)
    t1 = mm(mpo[...], one_hot(col_s * width + col_m == code_c)).astype(BF16)
    t2 = mm(one_hot(row_w * width + row_k == code_r), mpo[...]).astype(BF16)
    both = jnp.zeros((side, side), F32)
    for n in range(width):
        near = mm(one_hot(row_u * width + n == code_r), t1)
        both += near * mm(t2, one_hot(col_v * width + n == code_c))
    pair[...] = both.astype(BF16)

    add_far(1)
    spread_if(1, moves, True)
    finish(0, range(n_rs))
    home_left(0)
    spread_if(2, moves, False)
    relay(0)
    arrive(("right",), right)
    for i in range(cuts):
        acc[i, batch * pq:2 * batch * pq, :] = jnp.zeros((batch * pq, lanes), F32)

    def contract(stage, q, lo, n, at=0):
        ours = nl_in[stage, lo * width:(lo + n) * width, :]
        for t in range(pq // 2):
            mixed[t, at * width:(at + n) * width, :] = mm(ours, psi[q, t])

    def project(p):
        here = mixed[:, p * 2 * width:(p + 1) * 2 * width, :]
        tiles = []
        for i in range(2):
            one = here[:, i * width:(i + 1) * width, :].reshape(pq // 2 * width, 2 * lanes)
            tiles.append(jnp.concatenate([one[:, :lanes], one[:, lanes:]], axis=0))
        both = jnp.concatenate(tiles, axis=1).astype(BF16)
        out = mm(pair[...], both).astype(BF16)
        for i in range(2):
            where = pl.ds((p * 2 + i) * pq, pq)
            for k in range(width):
                proj[where, k * lanes:(k + 1) * lanes] = out[k * pq:(k + 1) * pq, i * lanes:(i + 1) * lanes]

    def environment(q):
        start = q * lanes if isinstance(q, int) else pl.multiple_of(q * lanes, lanes)
        return right[:, pl.ds(start, lanes), :].reshape(width * lanes, chi)

    def gathered(where):
        return jnp.concatenate([acc[i, where, :] for i in range(cuts)], axis=1)

    def strip_of(stage, q, lo=0, n=None, at=0):
        n = batch if n is None else n
        contract(stage, q, lo, n, at)
        for p in range(n // 2):
            project(at // 2 + p)
        total = mm(proj[at * pq:(at + n) * pq, :], environment(q))
        where = pl.ds((stage * batch + lo) * pq, n * pq)
        if not isinstance(q, int) or q > 0:
            total += gathered(where)
        for i in range(cuts):
            acc[i, where, :] = total[:, i * lanes:(i + 1) * lanes]

    def last_strip(stage, lo=0, n=None, at=0):
        n = batch if n is None else n
        q = cuts - 1
        contract(stage, q, lo, n, at)
        high = out_rows * pq
        for j in range(n // out_rows):
            for p in range(out_rows // 2):
                project(at // 2 + j * (out_rows // 2) + p)
            total = mm(proj[at * pq + j * high:at * pq + (j + 1) * high, :], environment(q))
            total += gathered(pl.ds((stage * batch + lo) * pq + j * high, high))
            out = total.reshape(out_rows, phys, phys, chi).astype(BF16)
            prod[stage, lo + j * out_rows:lo + (j + 1) * out_rows] = out
            home_product(stage, lo // out_rows + j)

    complete(0)
    spread_if(3, moves, False)
    for j in range(n_rs):
        high = pl.ds(j * rs_rows * width, rs_rows * width)
        arrive(("up", 0, j), nl_in.at[0, high, :])
    strip_of(0, 0)
    relay(1)
    complete(1)
    spread_if(3, stays, False)
    spread_reg(2)
    spread_reg(3)
    strip_of(0, 1)
    relay(2)
    complete(2)
    strip_of(0, 2)
    send_far(1, moves)
    relay(3)
    complete(3)
    send_far(1, stays)
    last_strip(0)
    def landed_rows(stage, parts):
        for j in parts:
            high = pl.ds(j * rs_rows * width, rs_rows * width)
            arrive(("up", stage, j), nl_in.at[stage, high, :])

    few = batch // 2
    early_parts, late_parts = range(n_rs // 2), range(n_rs // 2, n_rs)
    finish(1, early_parts)
    landed_rows(1, early_parts)

    strip_of(1, 0, 0, few)

    finish(1, late_parts)
    home_left(1)
    for q in range(1, cuts - 1):
        strip_of(1, q, 0, few, q % 2 * few)
    last_strip(1, 0, few, (cuts - 1) % 2 * few)
    landed_rows(1, late_parts)

    for q in range(cuts - 1):
        strip_of(1, q, few, few, q % 2 * few)
    last_strip(1, few, few, (cuts - 1) % 2 * few)
    finalize()


def fused(left_env, site, psi, right_env, mpo):
    _, rows, width, chi = left_env.shape
    phys = site.shape[2]
    pq = phys * phys
    group, cuts, batch = 16, 4, rows // 2
    lanes = chi // cuts
    small = phys * width
    table = mpo.transpose(0, 2, 3, 1)
    n_sems = 120
    any_spec = pl.BlockSpec(memory_space=pl.ANY)
    new_left, product = pl.pallas_call(
        functools.partial(kernel, (rows, width, phys, chi, group, cuts, batch)),
        out_shape=(
            jax.ShapeDtypeStruct((rows, width, chi), BF16),
            jax.ShapeDtypeStruct((rows, phys, phys, chi), BF16),
        ),
        in_specs=[any_spec] * 5,
        out_specs=(any_spec, any_spec),
        scratch_shapes=[
            pltpu.VMEM((rows, width, chi), BF16),
            pltpu.VMEM((rows, phys, chi), BF16),
            pltpu.VMEM((rows, phys, phys, chi), BF16),
            pltpu.VMEM((width, phys, phys, width), BF16),
            pltpu.VMEM((small, small), BF16),
            pltpu.VMEM((width, chi, chi), BF16),
            pltpu.VMEM((phys, rows, chi), BF16),
            pltpu.VMEM((cuts, pq // 2, rows, 2 * lanes), BF16),
            pltpu.VMEM((phys, chi, chi), BF16),
            pltpu.VMEM((chi, phys * rows), BF16),
            pltpu.VMEM((small * group, small * group), BF16),
            pltpu.VMEM((width * pq, width * pq), BF16),
            pltpu.VMEM((width, phys * rows, chi), BF16),
            pltpu.VMEM((width, chi, chi), BF16),
            pltpu.VMEM((2, 2, width, rows // 2, chi), BF16),
            pltpu.VMEM((2, width, rows // 2, chi), BF16),
            pltpu.VMEM((2, width, rows // 2, chi), BF16),
            pltpu.VMEM((2, rows // 2 * width, chi), BF16),
            pltpu.VMEM((2, rows // 2, width, chi), BF16),
            pltpu.VMEM((2, rows // 2 * width, chi), BF16),
            pltpu.VMEM((cuts, pq // 2, chi, 2 * lanes), BF16),
            pltpu.VMEM((pq // 2, batch * width, 2 * lanes), F32),
            pltpu.VMEM((batch * pq, width * lanes), BF16),
            pltpu.VMEM((2, rows // 2, phys, phys, chi), BF16),
            pltpu.VMEM((cuts, rows * pq, lanes), F32),
            pltpu.SemaphoreType.DMA((6,)),
            pltpu.SemaphoreType.DMA((n_sems,)),
            pltpu.SemaphoreType.DMA((n_sems,)),
            pltpu.SemaphoreType.REGULAR((2,)),
        ],
        compiler_params=pltpu.CompilerParams(
            collective_id=0, has_side_effects=True, vmem_limit_bytes=62 * 1024 * 1024
        ),
    )(left_env[0], site[0], psi[0], right_env[0], table)
    return settle(new_left, product)


def settle(*arrays):
    cut = 4

    def body(*refs):
        n = len(arrays)
        srcs, dsts, tmps, sem = refs[:n], refs[n:2 * n], refs[2 * n:3 * n], refs[3 * n]
        moves = []
        for i in reversed(range(n)):
            step = arrays[i].shape[0] // cut
            for j in range(cut):
                part = pl.ds(j * step, step)
                come = pltpu.make_async_copy(srcs[i].at[part], tmps[i].at[part], sem.at[0, i, j])
                go = pltpu.make_async_copy(tmps[i].at[part], dsts[i].at[0, part], sem.at[1, i, j])
                come.start()
                moves.append((come, go))
        for come, go in moves:
            come.wait()
            go.start()
        for _, go in moves:
            go.wait()

    spec = pl.BlockSpec(memory_space=pl.ANY)
    return pl.pallas_call(
        body,
        out_shape=tuple(jax.ShapeDtypeStruct((1,) + a.shape, a.dtype) for a in arrays),
        in_specs=[spec] * len(arrays),
        out_specs=(spec,) * len(arrays),
        scratch_shapes=[pltpu.VMEM(a.shape, a.dtype) for a in arrays]
        + [pltpu.SemaphoreType.DMA((2, len(arrays), cut))],
        compiler_params=pltpu.CompilerParams(vmem_limit_bytes=62 * 1024 * 1024),
    )(*arrays)


def shifted(block, axis, distance):
    devices = range(lax.axis_size(axis))
    route = [((i - distance) % len(devices), i) for i in devices]
    return lax.ppermute(block, axis, route)


def shards(left_env, site, psi, right_env, mpo):
    left = left_env[0]
    tensor = site[0]
    rows = tensor.shape[0]
    phys = tensor.shape[1]
    chi = tensor.shape[2]
    width = left.shape[1]
    pair_source = shifted(psi[0], "sec", 1)
    offset = lax.axis_index("bond") * rows
    whole_left, whole_site = (
        lax.all_gather(left, "bond", axis=0, tiled=True),
        lax.all_gather(tensor, "bond", axis=0, tiled=True),
    )
    own_cols = lax.dynamic_slice_in_dim(whole_site, offset, rows, 2)
    first = jnp.dot(
        whole_left.reshape(chi * width, chi),
        own_cols.reshape(chi, phys * rows),
        preferred_element_type=jnp.float32,
    )
    first = first.astype(jnp.bfloat16).reshape(chi, width, phys, rows)
    second = jnp.einsum("pmsb,mnsu->punb", first, mpo, preferred_element_type=jnp.float32).astype(
        jnp.bfloat16
    )
    fresh = lax.dot_general(
        whole_site.reshape(chi * phys, chi),
        second.reshape(chi * phys, width * rows),
        (((0,), (0,)), ((), ())),
        preferred_element_type=jnp.float32,
    )
    fresh = fresh.astype(jnp.bfloat16).reshape(chi, width, rows)
    new_left = lax.all_to_all(fresh, "bond", split_axis=0, concat_axis=2, tiled=True)
    left_source = shifted(new_left, "sec", 1)
    source_flat = left_source.reshape(rows * width, chi)
    pair = pair_source.reshape(rows, phys * phys * chi)
    mixed = jnp.dot(
        source_flat,
        lax.all_gather(pair, "bond", axis=0, tiled=True),
        preferred_element_type=jnp.float32,
    )
    mixed = mixed.astype(jnp.bfloat16).reshape(rows, width * phys * phys, chi)
    two_site = jnp.einsum("mnsu,nkvw->msvuwk", mpo, mpo, preferred_element_type=jnp.float32)
    two_site = two_site.astype(jnp.bfloat16).reshape(width * phys * phys, phys * phys * width)
    projected = jnp.einsum(
        "pqc,qr->prc", mixed, two_site, preferred_element_type=jnp.float32
    ).astype(jnp.bfloat16)
    env_right = right_env[0].reshape(width * chi, chi)
    result = jnp.dot(
        projected.reshape(rows * phys * phys, width * chi),
        env_right,
        preferred_element_type=jnp.float32,
    ).astype(jnp.bfloat16)
    return (new_left[None], result.reshape(1, rows, phys, phys, chi))


def solution(mesh):
    in_specs = (
        P("sec", "bond", None, None),
        P("sec", "bond", None, None),
        P("sec", "bond", None, None, None),
        P("sec", None, None, None),
        P(),
    )
    out_specs = (P("sec", "bond", None, None), P("sec", "bond", None, None, None))
    body = fused if mesh.shape["bond"] == 4 else shards
    return jax.shard_map(body, mesh=mesh, in_specs=in_specs, out_specs=out_specs, check_vma=False)
```
